512 devices in a mesh: row: 8 (over y, core), col: 8 (over z_lo), depth: 8 (over z_hi, x).
Axes of the slice: x: 4, y: 4, z: 16 (z_hi: 2, z_lo: 8; z = z_hi * 8 + z_lo), core: 2. Of those that a mesh axis runs over, the one named last changes fastest.
Arguments:
- tokens: bfloat16 [1024, 4096], P(('col', 'depth'), 'row'), may hold values from -6 to 6
- out_grad: bfloat16 [1024, 4096], P(('col', 'depth'), 'row'), may hold values from -2 to 2
- w_in: bfloat16 [4096, 14336], P('row', 'col'), may hold values from -0.09375 to 0.09375
- b_in: float32 [14336], P('col'), may hold values from -3 to 3
- w_out: bfloat16 [14336, 4096], P('col', 'row'), may hold values from -0.046875 to 0.046875
Outputs:
- block_out: bfloat16 [1024, 4096], P(('col', 'depth'), 'row')
- tokens_grad: bfloat16 [1024, 4096], P(('col', 'depth'), 'row')
- w_in_grad: bfloat16 [4096, 14336], P('row', ('col', 'depth'))
- w_out_grad: bfloat16 [14336, 4096], P(('col', 'depth'), 'row')
- b_in_grad: float32 [14336], P('col')
The draws below stay inside these ranges and needn't reach their ends.
All inputs are finite; a program needn't handle non-finite values.
Results may differ from the reference program's by a relative error of at most 0.005.
Values may be sent and summed in bfloat16 or wider, within the bound.
No kernel may reach another device: no remote copies, remote signals or barrier semaphores. Data moves between devices by JAX's collectives and lax.ppermute only.
A program may use at most 64 MiB of HBM per device.

```python
import jax
import jax.numpy as jnp

D = 4096
FF = 14336
TOKENS = 1024


def block_levels(rng, extent, pieces, smallest, top_value):
    def one(axis_at, shards_of):
        draws = jax.random.uniform(jax.random.fold_in(jax.random.fold_in(rng, 6), axis_at), (shards_of,), jnp.float32, smallest / len(pieces), top_value / len(pieces))
        return jnp.repeat(jnp.exp(draws), extent[axis_at] // shards_of).reshape((-1,) + (1,) * (len(extent) - axis_at - 1))

    loudness = one(*pieces[0])
    for cut in pieces[1:]:
        loudness = loudness * one(*cut)
    return loudness


def noise(own_key, extent, width, limit, split=(), held_as=jnp.bfloat16):
    loudness = block_levels(own_key, extent, split, -0.22, 0.18) if split else 1.0
    values = jax.random.normal(own_key, extent, jnp.float32) * width * loudness
    return jnp.minimum(jnp.maximum(values, -limit), limit).astype(held_as)


def setup_inputs(seed: int = 0) -> dict:
    key_of = jax.random.split(jax.random.key(seed), 6)
    return {
        "tokens": noise(key_of[0], (TOKENS, D), 1.0, 6.0, ((0, 64), (1, 8))),
        "out_grad": noise(key_of[1], (TOKENS, D), 0.3, 2.0, ((0, 64), (1, 8))),
        "w_in": noise(key_of[2], (D, FF), D ** -0.5, 0.09375, ((0, 8), (1, 8))),
        "b_in": noise(key_of[3], (FF,), 0.5, 3.0, ((0, 8),), jnp.float32),
        "w_out": noise(key_of[4], (FF, D), FF ** -0.5, 0.046875, ((0, 8), (1, 8))),
    }


root_coeff = 0.7978845608028654
cubic_coeff = 0.044715


def gelu_parts(pre_act):
    inner_arg = root_coeff * (pre_act + cubic_coeff * pre_act * pre_act * pre_act)
    tangent = jnp.tanh(inner_arg)
    gelu_value = 0.5 * pre_act * (1.0 + tangent)
    gelu_slope = 0.5 * (1.0 + tangent) + 0.5 * pre_act * (1.0 - tangent * tangent) * root_coeff * (1.0 + 3.0 * cubic_coeff * pre_act * pre_act)
    return gelu_value, gelu_slope


def reference(tokens, out_grad, w_in, b_in, w_out):
    pre_act = jnp.dot(tokens, w_in, preferred_element_type=jnp.float32) + b_in
    gelu_value, gelu_slope = gelu_parts(pre_act)
    hidden_act = gelu_value.astype(jnp.bfloat16)
    block_out = jnp.dot(hidden_act, w_out, preferred_element_type=jnp.float32).astype(jnp.bfloat16)
    act_grad = jnp.dot(out_grad, w_out.T, preferred_element_type=jnp.float32)
    pre_grad = act_grad * gelu_slope
    hidden_grad = pre_grad.astype(jnp.bfloat16)
    tokens_grad = jnp.dot(hidden_grad, w_in.T, preferred_element_type=jnp.float32).astype(jnp.bfloat16)
    w_in_grad = jnp.dot(tokens.T, hidden_grad, preferred_element_type=jnp.float32).astype(jnp.bfloat16)
    w_out_grad = jnp.dot(hidden_act.T, out_grad, preferred_element_type=jnp.float32).astype(jnp.bfloat16)
    b_in_grad = jnp.sum(pre_grad, axis=0)
    return block_out, tokens_grad, w_in_grad, w_out_grad, b_in_grad
```

```python
import jax
import jax.numpy as jnp
import numpy as np
from jax import lax
from jax.sharding import Mesh, PartitionSpec as P

root_coeff = 0.7978845608028654
cubic_coeff = 0.044715
f32 = jnp.float32
bf16 = jnp.bfloat16


def gelu_parts(pre_act):
    inner_arg = root_coeff * (pre_act + cubic_coeff * pre_act * pre_act * pre_act)
    tangent = jnp.tanh(inner_arg)
    gelu_value = 0.5 * pre_act * (1.0 + tangent)
    gelu_slope = 0.5 * (1.0 + tangent) + 0.5 * pre_act * (1.0 - tangent * tangent) * root_coeff * (
        1.0 + 3.0 * cubic_coeff * pre_act * pre_act
    )
    return (gelu_value, gelu_slope)


def dot_nt(a, b):
    return lax.dot_general(a, b, (((1,), (1,)), ((), ())), preferred_element_type=f32)


def dot_tn(a, b):
    return lax.dot_general(a, b, (((0,), (0,)), ((), ())), preferred_element_type=f32)


def dot_nn(a, b):
    return jnp.dot(a, b, preferred_element_type=f32)


def local(tokens, out_grad, w_in, b_in, w_out):
    y_n, core_n = lax.axis_size("y"), lax.axis_size("core")
    zl_n, zh_n, x_n = lax.axis_size("zl"), lax.axis_size("zh"), lax.axis_size("x")
    row_n, dep_n = y_n * core_n, zh_n * x_n
    tile, d_loc = tokens.shape
    f_loc = w_in.shape[1]
    part = f_loc // dep_n
    both = jnp.concatenate([tokens, out_grad], axis=0)
    zall = lax.all_gather(both, ("zh", "zl"), axis=0, tiled=True)
    others = [
        lax.ppermute(zall, "x", [(i, (i + k) % x_n) for i in range(x_n)]) for k in range(1, x_n)
    ]
    zs = zall.reshape(zh_n, y_n, core_n, 2, tile, d_loc)
    mine = lax.dynamic_index_in_dim(zs, lax.axis_index("zh"), 0, keepdims=False)
    mine = mine.transpose(2, 1, 0, 3, 4)
    plane_x = mine[0].reshape(row_n * tile, d_loc)
    plane_g = mine[1].reshape(row_n * tile, d_loc)
    pre = jnp.concatenate(
        [dot_nn(plane_x, w_in).astype(bf16), dot_nt(plane_g, w_out).astype(bf16)], axis=1
    )
    pre = lax.all_to_all(pre.reshape(core_n, y_n * tile, 2 * f_loc), "core", 0, 0)
    pre = jnp.sum(pre.astype(f32), axis=0).astype(bf16)
    pre = lax.all_to_all(pre.reshape(y_n, tile, 2 * f_loc), "y", 0, 0)
    pre = jnp.sum(pre.astype(f32), axis=0)
    value, slope = gelu_parts(pre[:, :f_loc] + b_in)
    pre_grad = pre[:, f_loc:] * slope
    b_part = jnp.sum(pre_grad, axis=0)
    act, hgrad = value.astype(bf16), pre_grad.astype(bf16)

    def hi_lo(v):
        hi = v.astype(bf16)
        return hi, (v - hi.astype(f32)).astype(bf16)

    b_rows = jnp.concatenate(hi_lo(b_part.reshape(dep_n // 2, 2 * part)), axis=0)
    send = jnp.concatenate(
        [
            act.reshape(tile, dep_n, part).transpose(1, 0, 2),
            hgrad.reshape(tile, dep_n, part).transpose(1, 0, 2),
        ],
        axis=2,
    )
    send = jnp.concatenate([send, jnp.broadcast_to(b_rows, (dep_n,) + b_rows.shape)], axis=1)
    got = lax.all_to_all(send, ("zh", "x"), 0, 0)
    plane = lax.all_gather(
        jnp.concatenate([act, hgrad], axis=1), ("y", "core"), axis=0, tiled=True
    )
    outs = jnp.concatenate(
        [dot_nn(plane[:, :f_loc], w_out).astype(bf16), dot_nt(plane[:, f_loc:], w_in).astype(bf16)],
        axis=1,
    )
    outs = lax.all_to_all(outs.reshape(zl_n, tile, 2 * d_loc), "zl", 0, 0)
    outs = jnp.sum(outs.astype(f32), axis=0).astype(bf16)
    half = dep_n // 2
    b_sum = jnp.sum(got[:, tile : tile + half].astype(f32) + got[:, tile + half :].astype(f32), axis=0)
    b_pair = jnp.concatenate(hi_lo(b_sum), axis=0)
    wsend = jnp.concatenate([got[:, :tile].reshape(dep_n * tile, 2 * part), b_pair], axis=0)
    wall = lax.all_gather(wsend, ("y", "core"), axis=0, tiled=False)
    b_all = wall[:, dep_n * tile :].astype(f32)
    b_in_grad = jnp.sum(b_all[:, :half] + b_all[:, half:], axis=0).reshape(f_loc)
    hid = wall[:, : dep_n * tile].reshape(zl_n, zh_n, x_n, tile, 2 * part)
    hid = hid.transpose(2, 1, 0, 3, 4).reshape(x_n, zh_n * zl_n * tile, 2 * part)
    my_x = lax.axis_index("x")
    w_in_grad = jnp.zeros((d_loc, part), f32)
    w_out_grad = jnp.zeros((part, d_loc), f32)
    for k, blk in enumerate([zall] + others):
        blk = blk.reshape(zh_n * zl_n, 2, tile, d_loc)
        xs = blk[:, 0].reshape(-1, d_loc)
        gs = blk[:, 1].reshape(-1, d_loc)
        hk = lax.dynamic_index_in_dim(hid, (my_x - k) % x_n, 0, keepdims=False)
        w_in_grad += dot_tn(xs, hk[:, part:])
        w_out_grad += dot_tn(hk[:, :part], gs)
    return (
        outs[:, :d_loc],
        outs[:, d_loc:],
        w_in_grad.astype(bf16),
        w_out_grad.astype(bf16),
        b_in_grad,
    )


def solution(mesh):
    fine = Mesh(mesh.devices.reshape(4, 2, 8, 2, 4), ("y", "core", "zl", "zh", "x"))
    tok = P(("zl", "zh", "x"), ("y", "core"))
    return jax.shard_map(
        local,
        mesh=fine,
        in_specs=(tok, tok, P(("y", "core"), "zl"), P("zl"), P("zl", ("y", "core"))),
        out_specs=(
            tok,
            tok,
            P(("y", "core"), ("zl", "zh", "x")),
            P(("zl", "zh", "x"), ("y", "core")),
            P("zl"),
        ),
        check_vma=False,
    )
```

```python
import functools

import jax
import jax.numpy as jnp
from jax import lax
from jax.experimental import pallas as pl
from jax.experimental.pallas import tpu as pltpu
from jax.sharding import Mesh, PartitionSpec as P

root_coeff = 0.7978845608028654
cubic_coeff = 0.044715
f32 = jnp.float32
bf16 = jnp.bfloat16
fine_names = ("y", "core", "zq", "zp", "zh", "x")
fine_shape = (4, 2, 4, 2, 2, 4)


def gelu_parts(pre_act):
    inner_arg = root_coeff * (pre_act + cubic_coeff * pre_act * pre_act * pre_act)
    tangent = jnp.tanh(inner_arg)
    gelu_value = 0.5 * pre_act * (1.0 + tangent)
    gelu_slope = 0.5 * (1.0 + tangent) + 0.5 * pre_act * (1.0 - tangent * tangent) * root_coeff * (
        1.0 + 3.0 * cubic_coeff * pre_act * pre_act
    )
    return (gelu_value, gelu_slope)


def dot_nt(a, b):
    return lax.dot_general(a, b, (((1,), (1,)), ((), ())), preferred_element_type=f32)


def dot_nn(a, b):
    return jnp.dot(a, b, preferred_element_type=f32)


def hi_lo(v):
    hi = v.astype(bf16).astype(f32)
    return hi, v - hi


def gelu_body(dep_n, recv_ref, bias_ref, hid_ref, send_ref):
    y_n, tile, wide = recv_ref.shape
    f_loc = wide // 2
    part = f_loc // dep_n
    pre = recv_ref[0].astype(f32)
    for j in range(1, y_n):
        pre = pre + recv_ref[j].astype(f32)
    value, slope = gelu_parts(pre[:, :f_loc] + bias_ref[...])
    pre_grad = pre[:, f_loc:] * slope
    hid = jnp.concatenate([value, pre_grad], axis=1).astype(bf16)
    for j in range(y_n):
        hid_ref[j] = hid
    rows = jnp.sum(pre_grad, axis=0, keepdims=True)
    hi, lo = hi_lo(rows)
    half = dep_n // 2
    extra = [v[:, j * 2 * part : (j + 1) * 2 * part] for v in (hi, lo) for j in range(half)]
    extra = jnp.concatenate(extra, axis=0).astype(bf16)
    for d in range(dep_n):
        cut = slice(d * part, (d + 1) * part)
        send_ref[d, :tile] = jnp.concatenate([value[:, cut], pre_grad[:, cut]], axis=1).astype(bf16)
        send_ref[d, tile:] = extra


def gelu_stage(recv, bias, dep_n):
    y_n, tile, wide = recv.shape
    return pl.pallas_call(
        functools.partial(gelu_body, dep_n),
        out_shape=(
            jax.ShapeDtypeStruct((y_n, tile, wide), bf16),
            jax.ShapeDtypeStruct((dep_n, tile + dep_n, wide // dep_n), bf16),
        ),
        name="gelu_stage",
    )(recv, bias.reshape(1, -1))


def repack_body(y_n, got_ref, out_ref):
    dep_n, tall, wide = got_ref.shape
    tile = tall - dep_n
    half = dep_n // 2
    blk = got_ref[:, :tile, :].reshape(dep_n * tile, wide)
    total = jnp.sum(got_ref[:, tile:, :].astype(f32), axis=0)
    hi, lo = hi_lo(total[:half] + total[half:])
    pair = jnp.concatenate([hi, lo], axis=0).astype(bf16)
    for j in range(y_n):
        out_ref[j, : dep_n * tile] = blk
        out_ref[j, dep_n * tile :] = pair


def repack_stage(got, y_n):
    dep_n, tall, wide = got.shape
    return pl.pallas_call(
        functools.partial(repack_body, y_n),
        out_shape=jax.ShapeDtypeStruct((y_n, dep_n * (tall - dep_n) + dep_n, wide), bf16),
        name="repack_stage",
    )(got)


def weight_body(
    place_ref, x0_ref, x1_ref, x2_ref, x3_ref, own_ref, oth_ref, win_ref, wout_ref, b_ref, h_ref
):
    y_n, tall, wide = own_ref.shape
    part = wide // 2
    half = b_ref.shape[1] // wide
    dep_n = 2 * half
    tile = (tall - dep_n) // dep_n
    x_refs = (x0_ref, x1_ref, x2_ref, x3_ref)
    x_n = len(x_refs)
    zh_n = dep_n // x_n
    my_core, my_x = place_ref[0], place_ref[1]
    total = jnp.zeros((dep_n, wide), f32)
    for j in range(y_n):
        total = total + own_ref[j, dep_n * tile :].astype(f32) + oth_ref[j, dep_n * tile :].astype(f32)
    total = total[:half] + total[half:]
    for j in range(half):
        b_ref[:, j * wide : (j + 1) * wide] = total[j : j + 1]
    acc_in = jnp.zeros(win_ref.shape, f32)
    acc_out = jnp.zeros(wout_ref.shape, f32)
    for k, x_ref in enumerate(x_refs):
        src_x = lax.rem(my_x + (x_n - k), x_n)
        for zh in range(zh_n):
            at = pl.multiple_of((zh * x_n + src_x) * tile, tile)
            for j in range(y_n):
                slot = (zh * y_n + j) * 2
                to_own = pl.multiple_of((slot + my_core) * tile, tile)
                to_oth = pl.multiple_of((slot + 1 - my_core) * tile, tile)
                h_ref[k, pl.ds(to_own, tile), :] = own_ref[j, pl.ds(at, tile), :]
                h_ref[k, pl.ds(to_oth, tile), :] = oth_ref[j, pl.ds(at, tile), :]
        turned = h_ref[k].T
        blk = x_ref[...].reshape(-1, 2, tile, x_ref.shape[-1])
        rows = blk.shape[0] * tile
        acc_out += dot_nn(turned[:part], blk[:, 1].reshape(rows, -1))
        acc_in += dot_nn(turned[part:], blk[:, 0].reshape(rows, -1))
    win_ref[...] = acc_in.astype(bf16)
    wout_ref[...] = acc_out.astype(bf16)


def weight_stage(place, chunks, own, oth, dep_n):
    y_n, tall, wide = own.shape
    d_loc = chunks[0].shape[-1]
    tokens_each = 2 * y_n * (dep_n // len(chunks)) * ((tall - dep_n) // dep_n)
    vmem = pl.BlockSpec(memory_space=pltpu.VMEM)
    return pl.pallas_call(
        weight_body,
        in_specs=[pl.BlockSpec(memory_space=pltpu.SMEM)] + [vmem] * 6,
        out_specs=(vmem, vmem, vmem),
        out_shape=(
            jax.ShapeDtypeStruct((wide // 2, d_loc), bf16),
            jax.ShapeDtypeStruct((wide // 2, d_loc), bf16),
            jax.ShapeDtypeStruct((1, wide * dep_n // 2), f32),
        ),
        scratch_shapes=[pltpu.VMEM((len(chunks), tokens_each, wide), bf16)],
        name="weight_stage",
    )(place, *chunks, own, oth)


def local(tokens, out_grad, w_in, b_in, w_out):
    y_n, x_n = lax.axis_size("y"), lax.axis_size("x")
    zh_n = lax.axis_size("zh")
    dep_n = zh_n * x_n
    tile, d_loc = tokens.shape
    f_loc = w_in.shape[1]
    my_core, my_x = lax.axis_index("core"), lax.axis_index("x")
    swap = [(0, 1), (1, 0)]

    both = jnp.concatenate([tokens, out_grad], axis=0)
    near = lax.ppermute(both, "zp", swap)
    first = lax.axis_index("zp") == 0
    pair = jnp.concatenate([jnp.where(first, both, near), jnp.where(first, near, both)], axis=0)
    zall = lax.all_gather(pair, ("zh", "zq"), axis=0, tiled=True)
    others = [
        lax.ppermute(zall, "x", [(i, (i + k) % x_n) for i in range(x_n)]) for k in range(1, x_n)
    ]
    mine = lax.dynamic_index_in_dim(
        zall.reshape(zh_n, y_n, 2, 2, tile, d_loc), lax.axis_index("zh"), 0, keepdims=False
    )

    def first_products(core):
        blk = lax.dynamic_index_in_dim(mine, core, 1, keepdims=False)
        return jnp.concatenate(
            [
                dot_nn(blk[:, 0].reshape(y_n * tile, d_loc), w_in),
                dot_nt(blk[:, 1].reshape(y_n * tile, d_loc), w_out),
            ],
            axis=1,
        )

    from_core = lax.ppermute(first_products(1 - my_core), "core", swap)
    pre = (first_products(my_core) + from_core).astype(bf16)
    pre = lax.all_to_all(pre.reshape(y_n, tile, 2 * f_loc), "y", 0, 0)
    hid, send = gelu_stage(pre, b_in, dep_n)
    own = lax.all_to_all(hid, "y", 0, 0)
    got = lax.all_to_all(send, ("zh", "x"), 0, 0)
    oth = lax.ppermute(own, "core", swap)

    def last_products(rows):
        rows = rows.reshape(y_n * tile, 2 * f_loc)
        res = jnp.concatenate(
            [dot_nn(rows[:, :f_loc], w_out).astype(bf16), dot_nt(rows[:, f_loc:], w_in).astype(bf16)],
            axis=1,
        )
        return res.reshape(y_n, tile, 2 * d_loc)

    res_own, res_oth = last_products(own), last_products(oth)
    even = my_core == 0
    outs = jnp.stack([jnp.where(even, res_own, res_oth), jnp.where(even, res_oth, res_own)], axis=1)
    outs = lax.all_to_all(outs.reshape(2 * y_n, tile, 2 * d_loc), ("zq", "zp"), 0, 0)
    outs = jnp.sum(outs.astype(f32), axis=0).astype(bf16)

    wown = lax.all_to_all(repack_stage(got, y_n), "y", 0, 0)
    woth = lax.ppermute(wown, "core", swap)
    place = jnp.stack([my_core, my_x])
    w_in_grad, w_out_grad, b_in_grad = weight_stage(place, [zall] + others, wown, woth, dep_n)
    return (outs[:, :d_loc], outs[:, d_loc:], w_in_grad.T, w_out_grad, b_in_grad.reshape(f_loc))


def solution(mesh):
    fine = Mesh(mesh.devices.reshape(fine_shape), fine_names)
    col = ("zq", "zp")
    row = ("y", "core")
    owner = ("zq", "zp", "zh", "x")
    tok = P(owner, row)
    return jax.shard_map(
        local,
        mesh=fine,
        in_specs=(tok, tok, P(row, col), P(col), P(col, row)),
        out_specs=(tok, tok, P(row, owner), P(owner, row), P(col)),
        check_vma=False,
    )
```

```python
import jax
import jax.numpy as jnp
from jax import lax
from jax.experimental import pallas as pl
from jax.experimental.pallas import tpu as pltpu
from jax.sharding import Mesh, PartitionSpec as P


root_coeff = 0.7978845608028654
cubic_coeff = 0.044715
f32 = jnp.float32
bf16 = jnp.bfloat16
fine_names = ("y", "core", "zq", "zp", "zh", "x")
fine_shape = (4, 2, 4, 2, 2, 4)


def gelu_parts(pre_act):
    inner_arg = root_coeff * (pre_act + cubic_coeff * pre_act * pre_act * pre_act)
    tangent = jnp.tanh(inner_arg)
    gelu_value = 0.5 * pre_act * (1.0 + tangent)
    gelu_slope = 0.5 * (1.0 + tangent) + 0.5 * pre_act * (1.0 - tangent * tangent) * root_coeff * (
        1.0 + 3.0 * cubic_coeff * pre_act * pre_act
    )
    return (gelu_value, gelu_slope)


def dot_nt(a, b):
    return lax.dot_general(a, b, (((1,), (1,)), ((), ())), preferred_element_type=f32)


def dot_nn(a, b):
    return jnp.dot(a, b, preferred_element_type=f32)


def hi_lo(v):
    hi = v.astype(bf16)
    return hi, (v - hi.astype(f32)).astype(bf16)


def weight_body(place_ref, x0_ref, x1_ref, x2_ref, x3_ref, hid_ref, win_ref, wout_ref, b_ref, h_ref):
    col_n, tall, wide = hid_ref.shape
    part = wide // 2
    half = b_ref.shape[1] // wide
    dep_n = 2 * half
    tile = (tall - dep_n) // dep_n
    x_refs = (x0_ref, x1_ref, x2_ref, x3_ref)
    x_n = len(x_refs)
    zh_n = dep_n // x_n
    my_x = place_ref[1]
    total = jnp.zeros((dep_n, wide), f32)
    for j in range(col_n):
        total = total + hid_ref[j, dep_n * tile :].astype(f32)
    total = total[:half] + total[half:]
    for j in range(half):
        b_ref[:, j * wide : (j + 1) * wide] = total[j : j + 1]
    acc_in = jnp.zeros(win_ref.shape, f32)
    acc_out = jnp.zeros(wout_ref.shape, f32)
    for k, x_ref in enumerate(x_refs):
        src_x = lax.rem(my_x + (x_n - k), x_n)
        for zh in range(zh_n):
            at = pl.multiple_of((zh * x_n + src_x) * tile, tile)
            for j in range(col_n):
                to = (zh * col_n + j) * tile
                h_ref[k, to : to + tile, :] = hid_ref[j, pl.ds(at, tile), :]
        turned = h_ref[k].T
        blk = x_ref[...].reshape(-1, 2, tile, x_ref.shape[-1])
        rows = blk.shape[0] * tile
        acc_out += dot_nn(turned[:part], blk[:, 1].reshape(rows, -1))
        acc_in += dot_nn(turned[part:], blk[:, 0].reshape(rows, -1))
    win_ref[...] = acc_in.astype(bf16)
    wout_ref[...] = acc_out.astype(bf16)


def weight_stage(place, chunks, hid, dep_n):
    _, _, wide = hid.shape
    d_loc = chunks[0].shape[-1]
    vmem = pl.BlockSpec(memory_space=pltpu.VMEM)
    return pl.pallas_call(
        weight_body,
        in_specs=[pl.BlockSpec(memory_space=pltpu.SMEM)] + [vmem] * 5,
        out_specs=(vmem, vmem, vmem),
        out_shape=(
            jax.ShapeDtypeStruct((wide // 2, d_loc), bf16),
            jax.ShapeDtypeStruct((wide // 2, d_loc), bf16),
            jax.ShapeDtypeStruct((1, wide * dep_n // 2), f32),
        ),
        scratch_shapes=[pltpu.VMEM((len(chunks), chunks[0].shape[0] // 2, wide), bf16)],
        name="weight_stage",
    )(place, *chunks, hid)


def step(tokens, out_grad, w_in, b_in, w_out):
    y_n, x_n = lax.axis_size("y"), lax.axis_size("x")
    zh_n = lax.axis_size("zh")
    dep_n = zh_n * x_n
    half = dep_n // 2
    tile, d_loc = tokens.shape
    f_loc = w_in.shape[1]
    part = f_loc // dep_n
    my_core, my_x = lax.axis_index("core"), lax.axis_index("x")
    swap = [(0, 1), (1, 0)]

    both = jnp.concatenate([tokens, out_grad], axis=0)
    zall = lax.all_gather(both, ("zh", "zq", "zp"), axis=0, tiled=True)
    others = []
    for k in range(1, x_n):
        others.append(lax.ppermute(zall, "x", [(i, (i + k) % x_n) for i in range(x_n)]))
    mine = lax.dynamic_index_in_dim(
        zall.reshape(zh_n, y_n, 2, 2, tile, d_loc), lax.axis_index("zh"), 0, keepdims=False
    )

    def first_products(core):
        blk = lax.dynamic_index_in_dim(mine, core, 1, keepdims=False)
        return jnp.concatenate(
            [
                dot_nn(blk[:, 0].reshape(y_n * tile, d_loc), w_in),
                dot_nt(blk[:, 1].reshape(y_n * tile, d_loc), w_out),
            ],
            axis=1,
        )

    from_core = lax.ppermute(first_products(1 - my_core), "core", swap)
    pre = (first_products(my_core) + from_core).astype(bf16)
    pre = lax.all_to_all(pre.reshape(y_n, tile, 2 * f_loc), "y", 0, 0)
    pre = jnp.sum(pre.astype(f32), axis=0)
    value, slope = gelu_parts(pre[:, :f_loc] + b_in)
    pre_grad = pre[:, f_loc:] * slope
    act, hgrad = value.astype(bf16), pre_grad.astype(bf16)
    hid = jnp.concatenate([act, hgrad], axis=1)
    b_rows = jnp.concatenate(hi_lo(jnp.sum(pre_grad, axis=0).reshape(half, 2 * part)), axis=0)
    send = jnp.concatenate(
        [
            act.reshape(tile, dep_n, part).transpose(1, 0, 2),
            hgrad.reshape(tile, dep_n, part).transpose(1, 0, 2),
        ],
        axis=2,
    )
    send = jnp.concatenate([send, jnp.broadcast_to(b_rows, (dep_n,) + b_rows.shape)], axis=1)
    got = lax.all_to_all(send, ("zh", "x"), 0, 0)
    rows = lax.all_gather(hid, ("y", "core"), axis=0, tiled=True)
    outs = jnp.concatenate(
        [dot_nn(rows[:, :f_loc], w_out).astype(bf16), dot_nt(rows[:, f_loc:], w_in).astype(bf16)],
        axis=1,
    )
    outs = lax.all_to_all(outs.reshape(2 * y_n, tile, 2 * d_loc), ("zq", "zp"), 0, 0)
    total = outs[0].astype(f32)
    for j in range(1, 2 * y_n):
        total = total + outs[j].astype(f32)
    block_out, tokens_grad = total[:, :d_loc].astype(bf16), total[:, d_loc:].astype(bf16)

    b_sum = jnp.sum(got[:, tile : tile + half].astype(f32) + got[:, tile + half :].astype(f32), axis=0)
    b_pair = jnp.concatenate(hi_lo(b_sum), axis=0)
    wsend = jnp.concatenate([got[:, :tile].reshape(dep_n * tile, 2 * part), b_pair], axis=0)
    wall = lax.all_gather(wsend, ("y", "core"), axis=0, tiled=False)
    place = jnp.stack([my_core, my_x])
    w_in_grad, w_out_grad, b_in_grad = weight_stage(place, [zall] + others, wall, dep_n)
    return (block_out, tokens_grad, w_in_grad.T, w_out_grad, b_in_grad.reshape(f_loc))


def solution(mesh):
    fine = Mesh(mesh.devices.reshape(fine_shape), fine_names)
    col = ("zq", "zp")
    row = ("y", "core")
    owner = ("zq", "zp", "zh", "x")
    tok = P(owner, row)
    return jax.shard_map(
        step,
        mesh=fine,
        in_specs=(tok, tok, P(row, col), P(col), P(col, row)),
        out_specs=(tok, tok, P(row, owner), P(owner, row), P(col)),
        check_vma=False,
    )
```

```python
import jax
import jax.numpy as jnp
from jax import lax
from jax.experimental import pallas as pl
from jax.experimental.pallas import tpu as pltpu
from jax.sharding import Mesh, PartitionSpec as P


root_coeff = 0.7978845608028654
cubic_coeff = 0.044715
f32 = jnp.float32
bf16 = jnp.bfloat16
fine_names = ("y", "core", "zq", "zp", "zh", "x")
fine_shape = (4, 2, 4, 2, 2, 4)


def gelu_parts(pre_act):
    inner_arg = root_coeff * (pre_act + cubic_coeff * pre_act * pre_act * pre_act)
    tangent = jnp.tanh(inner_arg)
    gelu_value = 0.5 * pre_act * (1.0 + tangent)
    gelu_slope = 0.5 * (1.0 + tangent) + 0.5 * pre_act * (1.0 - tangent * tangent) * root_coeff * (
        1.0 + 3.0 * cubic_coeff * pre_act * pre_act
    )
    return (gelu_value, gelu_slope)


def dot_nt(a, b):
    return lax.dot_general(a, b, (((1,), (1,)), ((), ())), preferred_element_type=f32)


def dot_nn(a, b):
    return jnp.dot(a, b, preferred_element_type=f32)


def hi_lo(v):
    hi = v.astype(bf16)
    return hi, (v - hi.astype(f32)).astype(bf16)


def weight_body(place_ref, x0_ref, x1_ref, x2_ref, x3_ref, hid_ref, win_ref, wout_ref, b_ref, h_ref):
    col_n, tall, wide = hid_ref.shape
    part = wide // 2
    half = b_ref.shape[1] // wide
    dep_n = 2 * half
    tile = (tall - dep_n) // dep_n
    x_refs = (x0_ref, x1_ref, x2_ref, x3_ref)
    x_n = len(x_refs)
    zh_n = dep_n // x_n
    my_x = place_ref[1]
    total = jnp.zeros((dep_n, wide), f32)
    for j in range(col_n):
        total = total + hid_ref[j, dep_n * tile :].astype(f32)
    total = total[:half] + total[half:]
    for j in range(half):
        b_ref[:, j * wide : (j + 1) * wide] = total[j : j + 1]
    acc_in = jnp.zeros(win_ref.shape, f32)
    acc_out = jnp.zeros(wout_ref.shape, f32)
    for k, x_ref in enumerate(x_refs):
        src_x = lax.rem(my_x + (x_n - k), x_n)
        for zh in range(zh_n):
            at = pl.multiple_of((zh * x_n + src_x) * tile, tile)
            for j in range(col_n):
                to = (zh * col_n + j) * tile
                h_ref[k, to : to + tile, :] = hid_ref[j, pl.ds(at, tile), :]
        turned = h_ref[k].T
        blk = x_ref[...].reshape(-1, 2, tile, x_ref.shape[-1])
        rows = blk.shape[0] * tile
        acc_out += dot_nn(turned[:part], blk[:, 1].reshape(rows, -1))
        acc_in += dot_nn(turned[part:], blk[:, 0].reshape(rows, -1))
    win_ref[...] = acc_in.astype(bf16)
    wout_ref[...] = acc_out.astype(bf16)


def in_vmem(x):
    return pltpu.with_memory_space_constraint(x, pltpu.VMEM)


def final_body(parts_ref, first_ref, second_ref):
    n, _, wide = parts_ref.shape
    total = parts_ref[0].astype(f32)
    for j in range(1, n):
        total = total + parts_ref[j].astype(f32)
    first_ref[...] = total[:, : wide // 2].astype(bf16)
    second_ref[...] = total[:, wide // 2 :].astype(bf16)


def final_stage(parts):
    _, tile, wide = parts.shape
    vmem = pl.BlockSpec(memory_space=pltpu.VMEM)
    half = jax.ShapeDtypeStruct((tile, wide // 2), bf16)
    return pl.pallas_call(
        final_body, in_specs=[vmem], out_specs=(vmem, vmem), out_shape=(half, half), name="final_stage"
    )(in_vmem(parts))


def weight_stage(place, chunks, hid, dep_n):
    _, _, wide = hid.shape
    d_loc = chunks[0].shape[-1]
    vmem = pl.BlockSpec(memory_space=pltpu.VMEM)
    return pl.pallas_call(
        weight_body,
        in_specs=[pl.BlockSpec(memory_space=pltpu.SMEM)] + [vmem] * 5,
        out_specs=(vmem, vmem, vmem),
        out_shape=(
            jax.ShapeDtypeStruct((wide // 2, d_loc), bf16),
            jax.ShapeDtypeStruct((wide // 2, d_loc), bf16),
            jax.ShapeDtypeStruct((1, wide * dep_n // 2), f32),
        ),
        scratch_shapes=[pltpu.VMEM((len(chunks), chunks[0].shape[0] // 2, wide), bf16)],
        name="weight_stage",
    )(place, *[in_vmem(c) for c in chunks], in_vmem(hid))


def step(tokens, out_grad, w_in, b_in, w_out):
    y_n, x_n = lax.axis_size("y"), lax.axis_size("x")
    zh_n = lax.axis_size("zh")
    dep_n = zh_n * x_n
    half = dep_n // 2
    tile, d_loc = tokens.shape
    f_loc = w_in.shape[1]
    part = f_loc // dep_n
    my_core, my_x = lax.axis_index("core"), lax.axis_index("x")
    swap = [(0, 1), (1, 0)]

    both = jnp.concatenate([tokens, out_grad], axis=0)
    zall = lax.all_gather(both, ("zh", "zq", "zp"), axis=0, tiled=True)
    others = []
    for k in range(1, x_n):
        others.append(lax.ppermute(zall, "x", [(i, (i + k) % x_n) for i in range(x_n)]))
    mine = lax.dynamic_index_in_dim(
        zall.reshape(zh_n, y_n, 2, 2, tile, d_loc), lax.axis_index("zh"), 0, keepdims=False
    )

    def first_products(core):
        blk = lax.dynamic_index_in_dim(mine, core, 1, keepdims=False)
        return jnp.concatenate(
            [
                dot_nn(blk[:, 0].reshape(y_n * tile, d_loc), w_in),
                dot_nt(blk[:, 1].reshape(y_n * tile, d_loc), w_out),
            ],
            axis=1,
        )

    from_core = lax.ppermute(first_products(1 - my_core), "core", swap)
    pre = (first_products(my_core) + from_core).astype(bf16)
    pre = lax.all_to_all(pre.reshape(y_n, tile, 2 * f_loc), "y", 0, 0)
    pre = jnp.sum(pre.astype(f32), axis=0)
    value, slope = gelu_parts(pre[:, :f_loc] + b_in)
    pre_grad = pre[:, f_loc:] * slope
    act, hgrad = value.astype(bf16), pre_grad.astype(bf16)
    hid = jnp.concatenate([act, hgrad], axis=1)
    b_rows = jnp.concatenate(hi_lo(jnp.sum(pre_grad, axis=0).reshape(half, 2 * part)), axis=0)
    send = jnp.concatenate(
        [
            act.reshape(tile, dep_n, part).transpose(1, 0, 2),
            hgrad.reshape(tile, dep_n, part).transpose(1, 0, 2),
        ],
        axis=2,
    )
    send = jnp.concatenate([send, jnp.broadcast_to(b_rows, (dep_n,) + b_rows.shape)], axis=1)
    got = lax.all_to_all(send, ("zh", "x"), 0, 0)
    rows = lax.all_gather(hid, ("y", "core"), axis=0, tiled=True)
    outs = jnp.concatenate(
        [dot_nn(rows[:, :f_loc], w_out).astype(bf16), dot_nt(rows[:, f_loc:], w_in).astype(bf16)],
        axis=1,
    )
    outs = lax.all_to_all(outs.reshape(2 * y_n, tile, 2 * d_loc), ("zq", "zp"), 0, 0)
    block_out, tokens_grad = final_stage(outs)

    b_sum = jnp.sum(got[:, tile : tile + half].astype(f32) + got[:, tile + half :].astype(f32), axis=0)
    b_pair = jnp.concatenate(hi_lo(b_sum), axis=0)
    wsend = jnp.concatenate([got[:, :tile].reshape(dep_n * tile, 2 * part), b_pair], axis=0)
    wall = lax.all_gather(wsend, ("y", "core"), axis=0, tiled=False)
    place = jnp.stack([my_core, my_x])
    w_in_grad, w_out_grad, b_in_grad = weight_stage(place, [zall] + others, wall, dep_n)
    return (block_out, tokens_grad, w_in_grad.T, w_out_grad, b_in_grad.reshape(f_loc))


def solution(mesh):
    fine = Mesh(mesh.devices.reshape(fine_shape), fine_names)
    col = ("zq", "zp")
    row = ("y", "core")
    owner = ("zq", "zp", "zh", "x")
    tok = P(owner, row)
    return jax.shard_map(
        step,
        mesh=fine,
        in_specs=(tok, tok, P(row, col), P(col), P(col, row)),
        out_specs=(tok, tok, P(row, owner), P(owner, row), P(col)),
        check_vma=False,
    )
```

```python
import jax
import jax.numpy as jnp
from jax import lax
from jax.experimental import pallas as pl
from jax.experimental.pallas import tpu as pltpu
from jax.sharding import Mesh, PartitionSpec as P


root_coeff = 0.7978845608028654
cubic_coeff = 0.044715
f32 = jnp.float32
bf16 = jnp.bfloat16
fine_names = ("y", "core", "zq", "zp", "zh", "x")
fine_shape = (4, 2, 4, 2, 2, 4)


def gelu_parts(pre_act):
    inner_arg = root_coeff * (pre_act + cubic_coeff * pre_act * pre_act * pre_act)
    tangent = jnp.tanh(inner_arg)
    gelu_value = 0.5 * pre_act * (1.0 + tangent)
    gelu_slope = 0.5 * (1.0 + tangent) + 0.5 * pre_act * (1.0 - tangent * tangent) * root_coeff * (
        1.0 + 3.0 * cubic_coeff * pre_act * pre_act
    )
    return (gelu_value, gelu_slope)


def dot_nt(a, b):
    return lax.dot_general(a, b, (((1,), (1,)), ((), ())), preferred_element_type=f32)


def dot_nn(a, b):
    return jnp.dot(a, b, preferred_element_type=f32)


def hi_lo(v):
    hi = v.astype(bf16)
    return hi, (v - hi.astype(f32)).astype(bf16)


def weight_body(x0_ref, x1_ref, x2_ref, x3_ref, hid_ref, win_ref, wout_ref, b_ref, flat_ref, h_ref, x_buf, sem):
    col_n, tall, wide = hid_ref.shape
    part = wide // 2
    half = flat_ref.shape[1] // wide
    dep_n = 2 * half
    tile = (tall - dep_n) // dep_n
    x_refs = (x0_ref, x1_ref, x2_ref, x3_ref)
    x_n = len(x_refs)
    zh_n = dep_n // x_n
    my_x = lax.axis_index("x")
    loads = [pltpu.make_async_copy(x_ref, x_buf.at[k], sem.at[k]) for k, x_ref in enumerate(x_refs)]
    for load in loads:
        load.start()
    total = jnp.zeros((dep_n, wide), f32)
    for j in range(col_n):
        total = total + hid_ref[j, dep_n * tile :].astype(f32)
    total = total[:half] + total[half:]
    for j in range(half):
        flat_ref[:, j * wide : (j + 1) * wide] = total[j : j + 1]
    for j in range(b_ref.shape[0]):
        b_ref[j : j + 1, :] = flat_ref[:, j * 128 : (j + 1) * 128]
    acc_in = jnp.zeros(win_ref.shape, f32)
    acc_out = jnp.zeros(wout_ref.shape, f32)
    for k, x_ref in enumerate(x_refs):
        src_x = lax.rem(my_x + (x_n - k), x_n)
        for zh in range(zh_n):
            at = pl.multiple_of((zh * x_n + src_x) * tile, tile)
            for j in range(col_n):
                to = (zh * col_n + j) * tile
                h_ref[k, to : to + tile, :] = hid_ref[j, pl.ds(at, tile), :]
        turned = h_ref[k].T
        loads[k].wait()
        blk = x_buf[k].reshape(-1, 2, tile, x_ref.shape[-1])
        rows = blk.shape[0] * tile
        acc_out += dot_nn(turned[:part], blk[:, 1].reshape(rows, -1))
        acc_in += dot_nn(turned[part:], blk[:, 0].reshape(rows, -1))
    win_ref[...] = acc_in.astype(bf16)
    wout_ref[...] = acc_out.astype(bf16)


def in_vmem(x):
    return pltpu.with_memory_space_constraint(x, pltpu.VMEM)


def final_body(parts_ref, first_ref, second_ref):
    n, _, wide = parts_ref.shape
    total = parts_ref[0].astype(f32)
    for j in range(1, n):
        total = total + parts_ref[j].astype(f32)
    first_ref[...] = total[:, : wide // 2].astype(bf16)
    second_ref[...] = total[:, wide // 2 :].astype(bf16)


def final_stage(parts):
    _, tile, wide = parts.shape
    vmem = pl.BlockSpec(memory_space=pltpu.VMEM)
    half = jax.ShapeDtypeStruct((tile, wide // 2), bf16)
    return pl.pallas_call(
        final_body, in_specs=[vmem], out_specs=(vmem, vmem), out_shape=(half, half), compiler_params=pltpu.CompilerParams(vmem_limit_bytes=4 << 20), name="final_stage"
    )(in_vmem(parts))


def weight_stage(chunks, hid, dep_n):
    _, _, wide = hid.shape
    d_loc = chunks[0].shape[-1]
    vmem = pl.BlockSpec(memory_space=pltpu.VMEM)
    return pl.pallas_call(
        weight_body,
        in_specs=[pl.BlockSpec(memory_space=pl.ANY)] * 4 + [vmem],
        out_specs=(vmem, vmem, vmem),
        out_shape=(
            jax.ShapeDtypeStruct((wide // 2, d_loc), bf16),
            jax.ShapeDtypeStruct((wide // 2, d_loc), bf16),
            jax.ShapeDtypeStruct((wide * dep_n // 256, 128), f32),
        ),
        scratch_shapes=[
            pltpu.VMEM((1, wide * dep_n // 2), f32),
            pltpu.VMEM((len(chunks), chunks[0].shape[0] // 2, wide), bf16),
            pltpu.VMEM((len(chunks),) + chunks[0].shape, bf16),
            pltpu.SemaphoreType.DMA((len(chunks),)),
        ],
        compiler_params=pltpu.CompilerParams(vmem_limit_bytes=16 << 20), name="weight_stage",
    )(*chunks, in_vmem(hid))


def step(tokens, out_grad, w_in, b_in, w_out):
    y_n, x_n = lax.axis_size("y"), lax.axis_size("x")
    zh_n = lax.axis_size("zh")
    dep_n = zh_n * x_n
    half = dep_n // 2
    tile, d_loc = tokens.shape
    f_loc = w_in.shape[1]
    part = f_loc // dep_n
    my_core = lax.axis_index("core")
    swap = [(0, 1), (1, 0)]

    both = jnp.concatenate([tokens, out_grad], axis=0)
    zall = lax.all_gather(both, ("zh", "zq", "zp"), axis=0, tiled=True)
    others = []
    for k in range(1, x_n):
        others.append(lax.ppermute(zall, "x", [(i, (i + k) % x_n) for i in range(x_n)]))
    mine = lax.dynamic_index_in_dim(
        zall.reshape(zh_n, y_n, 2, 2, tile, d_loc), lax.axis_index("zh"), 0, keepdims=False
    )

    def first_products(core):
        blk = lax.dynamic_index_in_dim(mine, core, 1, keepdims=False)
        return jnp.concatenate(
            [
                dot_nn(blk[:, 0].reshape(y_n * tile, d_loc), w_in),
                dot_nt(blk[:, 1].reshape(y_n * tile, d_loc), w_out),
            ],
            axis=1,
        )

    from_core = lax.ppermute(first_products(1 - my_core), "core", swap)
    pre = (first_products(my_core) + from_core).astype(bf16)
    pre = lax.all_to_all(pre.reshape(y_n, tile, 2 * f_loc), "y", 0, 0)
    pre = jnp.sum(pre.astype(f32), axis=0)
    value, slope = gelu_parts(pre[:, :f_loc] + b_in)
    pre_grad = pre[:, f_loc:] * slope
    act, hgrad = value.astype(bf16), pre_grad.astype(bf16)
    hid = jnp.concatenate([act, hgrad], axis=1)
    b_rows = jnp.concatenate(hi_lo(jnp.sum(pre_grad, axis=0).reshape(half, 2 * part)), axis=0)
    send = jnp.concatenate(
        [
            act.reshape(tile, dep_n, part).transpose(1, 0, 2),
            hgrad.reshape(tile, dep_n, part).transpose(1, 0, 2),
        ],
        axis=2,
    )
    send = jnp.concatenate([send, jnp.broadcast_to(b_rows, (dep_n,) + b_rows.shape)], axis=1)
    got = lax.all_to_all(send, ("zh", "x"), 0, 0)
    rows = lax.all_gather(hid, ("y", "core"), axis=0, tiled=True)
    outs = jnp.concatenate(
        [dot_nn(rows[:, :f_loc], w_out).astype(bf16), dot_nt(rows[:, f_loc:], w_in).astype(bf16)],
        axis=1,
    )
    outs = lax.all_to_all(outs.reshape(2 * y_n, tile, 2 * d_loc), ("zq", "zp"), 0, 0)
    block_out, tokens_grad = final_stage(outs)

    b_sum = jnp.sum(got[:, tile : tile + half].astype(f32) + got[:, tile + half :].astype(f32), axis=0)
    b_pair = jnp.concatenate(hi_lo(b_sum), axis=0)
    wsend = jnp.concatenate([got[:, :tile].reshape(dep_n * tile, 2 * part), b_pair], axis=0)
    wall = lax.all_gather(wsend, ("y", "core"), axis=0, tiled=False)
    w_in_grad, w_out_grad, b_in_grad = weight_stage([zall] + others, wall, dep_n)
    return (block_out, tokens_grad, w_in_grad.T, w_out_grad, b_in_grad.reshape(f_loc))


def solution(mesh):
    fine = Mesh(mesh.devices.reshape(fine_shape), fine_names)
    col = ("zq", "zp")
    row = ("y", "core")
    owner = ("zq", "zp", "zh", "x")
    tok = P(owner, row)
    return jax.shard_map(
        step,
        mesh=fine,
        in_specs=(tok, tok, P(row, col), P(col), P(col, row)),
        out_specs=(tok, tok, P(row, owner), P(owner, row), P(col)),
        check_vma=False,
    )
```

```python
import jax
import jax.numpy as jnp
from jax import lax
from jax.experimental import pallas as pl
from jax.experimental.pallas import tpu as pltpu
from jax.sharding import Mesh, PartitionSpec as P


root_coeff = 0.7978845608028654
cubic_coeff = 0.044715
f32 = jnp.float32
bf16 = jnp.bfloat16
fine_names = ("y", "core", "zq", "zp", "zh", "x")
fine_shape = (4, 2, 4, 2, 2, 4)


def gelu_parts(pre_act):
    inner_arg = root_coeff * (pre_act + cubic_coeff * pre_act * pre_act * pre_act)
    tangent = jnp.tanh(inner_arg)
    gelu_value = 0.5 * pre_act * (1.0 + tangent)
    gelu_slope = 0.5 * (1.0 + tangent) + 0.5 * pre_act * (1.0 - tangent * tangent) * root_coeff * (
        1.0 + 3.0 * cubic_coeff * pre_act * pre_act
    )
    return (gelu_value, gelu_slope)


def dot_nt(a, b):
    return lax.dot_general(a, b, (((1,), (1,)), ((), ())), preferred_element_type=f32)


def dot_nn(a, b):
    return jnp.dot(a, b, preferred_element_type=f32)


def hi_lo(v):
    hi = v.astype(bf16)
    return hi, (v - hi.astype(f32)).astype(bf16)


def weight_body(x0_ref, x1_ref, x2_ref, x3_ref, hid_ref, win_ref, wout_ref, b_ref, flat_ref, h_ref, x_buf, sem):
    col_n, tall, wide = hid_ref.shape
    part = wide // 2
    half = flat_ref.shape[1] // wide
    dep_n = 2 * half
    tile = (tall - dep_n) // dep_n
    x_refs = (x0_ref, x1_ref, x2_ref, x3_ref)
    x_n = len(x_refs)
    zh_n = dep_n // x_n
    my_x = lax.axis_index("x")
    loads = [pltpu.make_async_copy(x_ref, x_buf.at[k], sem.at[k]) for k, x_ref in enumerate(x_refs)]
    for load in loads:
        load.start()
    total = jnp.zeros((dep_n, wide), f32)
    for j in range(col_n):
        total = total + hid_ref[j, dep_n * tile :].astype(f32)
    total = total[:half] + total[half:]
    for j in range(half):
        flat_ref[:, j * wide : (j + 1) * wide] = total[j : j + 1]
    for j in range(b_ref.shape[0]):
        b_ref[j : j + 1, :] = flat_ref[:, j * 128 : (j + 1) * 128]
    acc_in = jnp.zeros(win_ref.shape, f32)
    acc_out = jnp.zeros(wout_ref.shape, f32)
    for k, x_ref in enumerate(x_refs):
        src_x = lax.rem(my_x + (x_n - k), x_n)
        for zh in range(zh_n):
            at = pl.multiple_of((zh * x_n + src_x) * tile, tile)
            for j in range(col_n):
                to = (zh * col_n + j) * tile
                h_ref[k, to : to + tile, :] = hid_ref[j, pl.ds(at, tile), :]
        turned = h_ref[k].T
        loads[k].wait()
        blk = x_buf[k].reshape(-1, 2, tile, x_ref.shape[-1])
        rows = blk.shape[0] * tile
        acc_out += dot_nn(turned[:part], blk[:, 1].reshape(rows, -1))
        acc_in += dot_nn(turned[part:], blk[:, 0].reshape(rows, -1))
    win_ref[...] = acc_in.astype(bf16)
    wout_ref[...] = acc_out.astype(bf16)


def in_vmem(x):
    return pltpu.with_memory_space_constraint(x, pltpu.VMEM)


def final_body(parts_ref, first_ref, second_ref):
    n, _, wide = parts_ref.shape
    total = parts_ref[0].astype(f32)
    for j in range(1, n):
        total = total + parts_ref[j].astype(f32)
    first_ref[...] = total[:, : wide // 2].astype(bf16)
    second_ref[...] = total[:, wide // 2 :].astype(bf16)


def final_stage(parts):
    _, tile, wide = parts.shape
    vmem = pl.BlockSpec(memory_space=pltpu.VMEM)
    half = jax.ShapeDtypeStruct((tile, wide // 2), bf16)
    return pl.pallas_call(
        final_body, in_specs=[vmem], out_specs=(vmem, vmem), out_shape=(half, half), compiler_params=pltpu.CompilerParams(vmem_limit_bytes=4 << 20), name="final_stage"
    )(in_vmem(parts))


def weight_stage(chunks, hid, dep_n):
    _, _, wide = hid.shape
    d_loc = chunks[0].shape[-1]
    vmem = pl.BlockSpec(memory_space=pltpu.VMEM)
    return pl.pallas_call(
        weight_body,
        in_specs=[pl.BlockSpec(memory_space=pl.ANY)] * 4 + [vmem],
        out_specs=(vmem, vmem, vmem),
        out_shape=(
            jax.ShapeDtypeStruct((wide // 2, d_loc), bf16),
            jax.ShapeDtypeStruct((wide // 2, d_loc), bf16),
            jax.ShapeDtypeStruct((wide * dep_n // 256, 128), f32),
        ),
        scratch_shapes=[
            pltpu.VMEM((1, wide * dep_n // 2), f32),
            pltpu.VMEM((len(chunks), chunks[0].shape[0] // 2, wide), bf16),
            pltpu.VMEM((len(chunks),) + chunks[0].shape, bf16),
            pltpu.SemaphoreType.DMA((len(chunks),)),
        ],
        compiler_params=pltpu.CompilerParams(vmem_limit_bytes=16 << 20), name="weight_stage",
    )(*chunks, in_vmem(hid))


def step(tokens, out_grad, w_in, b_in, w_out):
    y_n, x_n = lax.axis_size("y"), lax.axis_size("x")
    zh_n, row_n = lax.axis_size("zh"), y_n * lax.axis_size("core")
    dep_n = zh_n * x_n
    half = dep_n // 2
    tile, d_loc = tokens.shape
    f_loc = w_in.shape[1]
    part = f_loc // dep_n
    both = jnp.concatenate([tokens, out_grad], axis=0)
    zall = lax.all_gather(both, ("zh", "zq", "zp"), axis=0, tiled=True)
    others = []
    for k in range(1, x_n):
        others.append(lax.ppermute(zall, "x", [(i, (i + k) % x_n) for i in range(x_n)]))
    mine = lax.dynamic_index_in_dim(
        zall.reshape(zh_n, row_n, 2, tile, d_loc), lax.axis_index("zh"), 0, keepdims=False
    )
    pre_part = dot_nn(mine[:, 0].reshape(row_n * tile, d_loc), w_in).astype(bf16)
    grad_part = dot_nt(mine[:, 1].reshape(row_n * tile, d_loc), w_out).astype(bf16)
    pre = jnp.concatenate([pre_part, grad_part], axis=1)
    pre = lax.all_to_all(pre.reshape(row_n, tile, 2 * f_loc), ("y", "core"), 0, 0)
    pre = jnp.sum(pre.astype(f32), axis=0)
    value, slope = gelu_parts(pre[:, :f_loc] + b_in)
    pre_grad = pre[:, f_loc:] * slope
    act, hgrad = value.astype(bf16), pre_grad.astype(bf16)
    hid = jnp.concatenate([act, hgrad], axis=1)
    b_rows = jnp.concatenate(hi_lo(jnp.sum(pre_grad, axis=0).reshape(half, 2 * part)), axis=0)
    send = jnp.concatenate(
        [
            act.reshape(tile, dep_n, part).transpose(1, 0, 2),
            hgrad.reshape(tile, dep_n, part).transpose(1, 0, 2),
        ],
        axis=2,
    )
    send = jnp.concatenate([send, jnp.broadcast_to(b_rows, (dep_n,) + b_rows.shape)], axis=1)
    got = lax.all_to_all(send, ("zh", "x"), 0, 0)
    rows = lax.all_gather(hid, ("y", "core"), axis=0, tiled=True)
    outs = jnp.concatenate(
        [dot_nn(rows[:, :f_loc], w_out).astype(bf16), dot_nt(rows[:, f_loc:], w_in).astype(bf16)],
        axis=1,
    )
    outs = lax.all_to_all(outs.reshape(row_n, tile, 2 * d_loc), ("zq", "zp"), 0, 0)
    block_out, tokens_grad = final_stage(outs)

    b_sum = jnp.sum(got[:, tile : tile + half].astype(f32) + got[:, tile + half :].astype(f32), axis=0)
    b_pair = jnp.concatenate(hi_lo(b_sum), axis=0)
    wsend = jnp.concatenate([got[:, :tile].reshape(dep_n * tile, 2 * part), b_pair], axis=0)
    wall = lax.all_gather(wsend, ("y", "core"), axis=0, tiled=False)
    w_in_grad, w_out_grad, b_in_grad = weight_stage([zall] + others, wall, dep_n)
    return (block_out, tokens_grad, w_in_grad.T, w_out_grad, b_in_grad.reshape(f_loc))


def solution(mesh):
    fine = Mesh(mesh.devices.reshape(fine_shape), fine_names)
    col = ("zq", "zp")
    row = ("y", "core")
    owner = ("zq", "zp", "zh", "x")
    tok = P(owner, row)
    return jax.shard_map(
        step,
        mesh=fine,
        in_specs=(tok, tok, P(row, col), P(col), P(col, row)),
        out_specs=(tok, tok, P(row, owner), P(owner, row), P(col)),
        check_vma=False,
    )
```

```python
import functools

import jax
import jax.numpy as jnp
from jax import lax
from jax.experimental import pallas as pl
from jax.experimental.pallas import tpu as pltpu
from jax.sharding import Mesh, PartitionSpec as P


root_coeff = 0.7978845608028654
cubic_coeff = 0.044715
f32 = jnp.float32
bf16 = jnp.bfloat16
fine_names = ("y", "core", "zq", "zp", "zh", "x")
fine_shape = (4, 2, 4, 2, 2, 4)


def gelu_parts(pre_act):
    inner_arg = root_coeff * (pre_act + cubic_coeff * pre_act * pre_act * pre_act)
    tangent = jnp.tanh(inner_arg)
    gelu_value = 0.5 * pre_act * (1.0 + tangent)
    gelu_slope = 0.5 * (1.0 + tangent) + 0.5 * pre_act * (1.0 - tangent * tangent) * root_coeff * (
        1.0 + 3.0 * cubic_coeff * pre_act * pre_act
    )
    return (gelu_value, gelu_slope)


def dot_nt(a, b):
    return lax.dot_general(a, b, (((1,), (1,)), ((), ())), preferred_element_type=f32)


def dot_nn(a, b):
    return jnp.dot(a, b, preferred_element_type=f32)


def hi_lo(v):
    hi = v.astype(bf16)
    return hi, (v - hi.astype(f32)).astype(bf16)


def gelu_body(dep_n, recv_ref, bias_ref, hid_ref, send_ref):
    y_n, tile, wide = recv_ref.shape
    f_loc = wide // 2
    part = f_loc // dep_n
    half = dep_n // 2
    pre = recv_ref[0].astype(f32)
    for j in range(1, y_n):
        pre = pre + recv_ref[j].astype(f32)
    bias = jnp.concatenate([bias_ref[j : j + 1, :] for j in range(bias_ref.shape[0])], axis=1)
    value, slope = gelu_parts(pre[:, :f_loc] + bias)
    pre_grad = pre[:, f_loc:] * slope
    hid_ref[:, :f_loc] = value.astype(bf16)
    hid_ref[:, f_loc:] = pre_grad.astype(bf16)
    rows = jnp.sum(pre_grad, axis=0, keepdims=True)
    high = rows.astype(bf16).astype(f32)
    extra = [v[:, j * 2 * part : (j + 1) * 2 * part] for v in (high, rows - high) for j in range(half)]
    extra = jnp.concatenate(extra, axis=0).astype(bf16)
    for d in range(dep_n):
        cut = slice(d * part, (d + 1) * part)
        send_ref[d, :tile] = jnp.concatenate([value[:, cut], pre_grad[:, cut]], axis=1).astype(bf16)
        send_ref[d, tile:] = extra


def gelu_stage(recv, bias, dep_n):
    _, tile, wide = recv.shape
    vmem = pl.BlockSpec(memory_space=pltpu.VMEM)
    return pl.pallas_call(
        functools.partial(gelu_body, dep_n),
        in_specs=[vmem, vmem],
        out_specs=(vmem, vmem),
        out_shape=(
            jax.ShapeDtypeStruct((tile, wide), bf16),
            jax.ShapeDtypeStruct((dep_n, tile + dep_n, wide // dep_n), bf16),
        ),
        compiler_params=pltpu.CompilerParams(vmem_limit_bytes=8 << 20),
        name="gelu_stage",
    )(in_vmem(recv), bias.reshape(-1, 128))


def weight_body(x0_ref, x1_ref, x2_ref, x3_ref, hid_ref, win_ref, wout_ref, b_ref, flat_ref, h_ref, x_buf, sem):
    col_n, tall, wide = hid_ref.shape
    part = wide // 2
    half = flat_ref.shape[1] // wide
    dep_n = 2 * half
    tile = (tall - dep_n) // dep_n
    x_refs = (x0_ref, x1_ref, x2_ref, x3_ref)
    x_n = len(x_refs)
    zh_n = dep_n // x_n
    my_x = lax.axis_index("x")
    loads = [pltpu.make_async_copy(x_ref, x_buf.at[k], sem.at[k]) for k, x_ref in enumerate(x_refs)]
    for load in loads:
        load.start()
    total = jnp.zeros((dep_n, wide), f32)
    for j in range(col_n):
        total = total + hid_ref[j, dep_n * tile :].astype(f32)
    total = total[:half] + total[half:]
    for j in range(half):
        flat_ref[:, j * wide : (j + 1) * wide] = total[j : j + 1]
    for j in range(b_ref.shape[0]):
        b_ref[j : j + 1, :] = flat_ref[:, j * 128 : (j + 1) * 128]
    acc_in = jnp.zeros(win_ref.shape, f32)
    acc_out = jnp.zeros(wout_ref.shape, f32)
    for k, x_ref in enumerate(x_refs):
        src_x = lax.rem(my_x + (x_n - k), x_n)
        for zh in range(zh_n):
            at = pl.multiple_of((zh * x_n + src_x) * tile, tile)
            for j in range(col_n):
                to = (zh * col_n + j) * tile
                h_ref[k, to : to + tile, :] = hid_ref[j, pl.ds(at, tile), :]
        turned = h_ref[k].T
        loads[k].wait()
        blk = x_buf[k].reshape(-1, 2, tile, x_ref.shape[-1])
        rows = blk.shape[0] * tile
        acc_out += dot_nn(turned[:part], blk[:, 1].reshape(rows, -1))
        acc_in += dot_nn(turned[part:], blk[:, 0].reshape(rows, -1))
    win_ref[...] = acc_in.astype(bf16)
    wout_ref[...] = acc_out.astype(bf16)


def in_vmem(x):
    return pltpu.with_memory_space_constraint(x, pltpu.VMEM)


def final_body(parts_ref, first_ref, second_ref):
    n, _, wide = parts_ref.shape
    total = parts_ref[0].astype(f32)
    for j in range(1, n):
        total = total + parts_ref[j].astype(f32)
    first_ref[...] = total[:, : wide // 2].astype(bf16)
    second_ref[...] = total[:, wide // 2 :].astype(bf16)


def final_stage(parts):
    _, tile, wide = parts.shape
    vmem = pl.BlockSpec(memory_space=pltpu.VMEM)
    half = jax.ShapeDtypeStruct((tile, wide // 2), bf16)
    return pl.pallas_call(
        final_body, in_specs=[vmem], out_specs=(vmem, vmem), out_shape=(half, half), compiler_params=pltpu.CompilerParams(vmem_limit_bytes=4 << 20), name="final_stage"
    )(in_vmem(parts))


def weight_stage(chunks, hid, dep_n):
    _, _, wide = hid.shape
    d_loc = chunks[0].shape[-1]
    vmem = pl.BlockSpec(memory_space=pltpu.VMEM)
    return pl.pallas_call(
        weight_body,
        in_specs=[pl.BlockSpec(memory_space=pl.ANY)] * 4 + [vmem],
        out_specs=(vmem, vmem, vmem),
        out_shape=(
            jax.ShapeDtypeStruct((wide // 2, d_loc), bf16),
            jax.ShapeDtypeStruct((wide // 2, d_loc), bf16),
            jax.ShapeDtypeStruct((wide * dep_n // 256, 128), f32),
        ),
        scratch_shapes=[
            pltpu.VMEM((1, wide * dep_n // 2), f32),
            pltpu.VMEM((len(chunks), chunks[0].shape[0] // 2, wide), bf16),
            pltpu.VMEM((len(chunks),) + chunks[0].shape, bf16),
            pltpu.SemaphoreType.DMA((len(chunks),)),
        ],
        compiler_params=pltpu.CompilerParams(vmem_limit_bytes=16 << 20), name="weight_stage",
    )(*chunks, in_vmem(hid))


def step(tokens, out_grad, w_in, b_in, w_out):
    y_n, x_n = lax.axis_size("y"), lax.axis_size("x")
    zh_n = lax.axis_size("zh")
    dep_n = zh_n * x_n
    half = dep_n // 2
    tile, d_loc = tokens.shape
    f_loc = w_in.shape[1]
    part = f_loc // dep_n
    my_core = lax.axis_index("core")
    swap = [(0, 1), (1, 0)]

    both = jnp.concatenate([tokens, out_grad], axis=0)
    zall = lax.all_gather(both, ("zh", "zq", "zp"), axis=0, tiled=True)
    others = []
    for k in range(1, x_n):
        others.append(lax.ppermute(zall, "x", [(i, (i + k) % x_n) for i in range(x_n)]))
    mine = lax.dynamic_index_in_dim(
        zall.reshape(zh_n, y_n, 2, 2, tile, d_loc), lax.axis_index("zh"), 0, keepdims=False
    )

    def first_products(core):
        blk = lax.dynamic_index_in_dim(mine, core, 1, keepdims=False)
        part_in = dot_nn(blk[:, 0].reshape(y_n * tile, d_loc), w_in)
        part_out = dot_nt(blk[:, 1].reshape(y_n * tile, d_loc), w_out)
        return jnp.concatenate([part_in, part_out], axis=1)

    from_core = lax.ppermute(first_products(1 - my_core), "core", swap)
    pre = (first_products(my_core) + from_core).astype(bf16)
    pre = lax.all_to_all(pre.reshape(y_n, tile, 2 * f_loc), "y", 0, 0)
    hid, send = gelu_stage(pre, b_in, dep_n)
    got = lax.all_to_all(send, ("zh", "x"), 0, 0)
    rows = lax.all_gather(hid, ("y", "core"), axis=0, tiled=True)
    outs = jnp.concatenate(
        [dot_nn(rows[:, :f_loc], w_out).astype(bf16), dot_nt(rows[:, f_loc:], w_in).astype(bf16)],
        axis=1,
    )
    outs = lax.all_to_all(outs.reshape(2 * y_n, tile, 2 * d_loc), ("zq", "zp"), 0, 0)
    block_out, tokens_grad = final_stage(outs)

    b_sum = jnp.sum(got[:, tile : tile + half].astype(f32) + got[:, tile + half :].astype(f32), axis=0)
    b_pair = jnp.concatenate(hi_lo(b_sum), axis=0)
    wsend = jnp.concatenate([got[:, :tile].reshape(dep_n * tile, 2 * part), b_pair], axis=0)
    wall = lax.all_gather(wsend, ("y", "core"), axis=0, tiled=False)
    w_in_grad, w_out_grad, b_in_grad = weight_stage([zall] + others, wall, dep_n)
    return (block_out, tokens_grad, w_in_grad.T, w_out_grad, b_in_grad.reshape(f_loc))


def solution(mesh):
    fine = Mesh(mesh.devices.reshape(fine_shape), fine_names)
    col = ("zq", "zp")
    row = ("y", "core")
    owner = ("zq", "zp", "zh", "x")
    tok = P(owner, row)
    return jax.shard_map(
        step,
        mesh=fine,
        in_specs=(tok, tok, P(row, col), P(col), P(col, row)),
        out_specs=(tok, tok, P(row, owner), P(owner, row), P(col)),
        check_vma=False,
    )
```

```python
import functools

import jax
import jax.numpy as jnp
from jax import lax
from jax.experimental import pallas as pl
from jax.experimental.pallas import tpu as pltpu
from jax.sharding import Mesh, PartitionSpec as P


root_coeff = 0.7978845608028654
cubic_coeff = 0.044715
f32 = jnp.float32
bf16 = jnp.bfloat16
fine_names = ("y", "core", "zq", "zp", "zh", "x")
fine_shape = (4, 2, 4, 2, 2, 4)


def gelu_parts(pre_act):
    inner_arg = root_coeff * (pre_act + cubic_coeff * pre_act * pre_act * pre_act)
    tangent = jnp.tanh(inner_arg)
    gelu_value = 0.5 * pre_act * (1.0 + tangent)
    gelu_slope = 0.5 * (1.0 + tangent) + 0.5 * pre_act * (1.0 - tangent * tangent) * root_coeff * (
        1.0 + 3.0 * cubic_coeff * pre_act * pre_act
    )
    return (gelu_value, gelu_slope)


def dot_nt(a, b):
    return lax.dot_general(a, b, (((1,), (1,)), ((), ())), preferred_element_type=f32)


def dot_nn(a, b):
    return jnp.dot(a, b, preferred_element_type=f32)


def hi_lo(v):
    hi = v.astype(bf16)
    return hi, (v - hi.astype(f32)).astype(bf16)


def gelu_body(zh_n, x_n, recv_ref, bias_ref, hid_ref, send_ref, both_ref):
    y_n, rows_n, wide = recv_ref.shape
    f_loc = wide // 2
    tile = rows_n // zh_n
    far = f_loc // zh_n
    part = far // x_n
    half = f_loc // (2 * part)
    my_zh = lax.axis_index("zh")
    pre = recv_ref[0].astype(f32)
    for j in range(1, y_n):
        pre = pre + recv_ref[j].astype(f32)
    bias = jnp.concatenate([bias_ref[j : j + 1, :] for j in range(bias_ref.shape[0])], axis=1)
    value, slope = gelu_parts(pre[:, :f_loc] + bias)
    pre_grad = pre[:, f_loc:] * slope
    both_ref[:, :f_loc] = value.astype(bf16)
    both_ref[:, f_loc:] = pre_grad.astype(bf16)
    hid_ref[...] = both_ref[pl.ds(pl.multiple_of(my_zh * tile, tile), tile), :]
    rows = jnp.sum(pre_grad, axis=0, keepdims=True)
    high = rows.astype(bf16).astype(f32)
    extra = [v[:, j * 2 * part : (j + 1) * 2 * part] for v in (high, rows - high) for j in range(half)]
    extra = jnp.concatenate(extra, axis=0).astype(bf16)
    near = my_zh == 0
    value = jnp.where(near, value[:, :far], value[:, far:])
    pre_grad = jnp.where(near, pre_grad[:, :far], pre_grad[:, far:])
    for x in range(x_n):
        cut = slice(x * part, (x + 1) * part)
        send_ref[x, :rows_n] = jnp.concatenate([value[:, cut], pre_grad[:, cut]], axis=1).astype(bf16)
        send_ref[x, rows_n:] = extra


def gelu_stage(recv, bias, zh_n, x_n):
    _, rows_n, wide = recv.shape
    dep_n = zh_n * x_n
    vmem = pl.BlockSpec(memory_space=pltpu.VMEM)
    return pl.pallas_call(
        functools.partial(gelu_body, zh_n, x_n),
        in_specs=[vmem, vmem],
        out_specs=(vmem, vmem),
        out_shape=(
            jax.ShapeDtypeStruct((rows_n // zh_n, wide), bf16),
            jax.ShapeDtypeStruct((x_n, rows_n + dep_n, wide // dep_n), bf16),
        ),
        scratch_shapes=[pltpu.VMEM((rows_n, wide), bf16)],
        compiler_params=pltpu.CompilerParams(vmem_limit_bytes=16 << 20),
        name="gelu_stage",
    )(in_vmem(recv), bias.reshape(-1, 128))


def weight_body(x0_ref, x1_ref, x2_ref, x3_ref, hid_ref, win_ref, wout_ref, b_ref, flat_ref, h_ref, x_buf, sem):
    col_n, tall, wide = hid_ref.shape
    part = wide // 2
    half = flat_ref.shape[1] // wide
    dep_n = 2 * half
    tile = (tall - dep_n) // dep_n
    x_refs = (x0_ref, x1_ref, x2_ref, x3_ref)
    x_n = len(x_refs)
    zh_n = dep_n // x_n
    my_x = lax.axis_index("x")
    loads = [pltpu.make_async_copy(x_ref, x_buf.at[k], sem.at[k]) for k, x_ref in enumerate(x_refs)]
    for load in loads:
        load.start()
    total = jnp.zeros((dep_n, wide), f32)
    for j in range(col_n):
        total = total + hid_ref[j, dep_n * tile :].astype(f32)
    total = total[:half] + total[half:]
    for j in range(half):
        flat_ref[:, j * wide : (j + 1) * wide] = total[j : j + 1]
    for j in range(b_ref.shape[0]):
        b_ref[j : j + 1, :] = flat_ref[:, j * 128 : (j + 1) * 128]
    acc_in = jnp.zeros(win_ref.shape, f32)
    acc_out = jnp.zeros(wout_ref.shape, f32)
    for k, x_ref in enumerate(x_refs):
        src_x = lax.rem(my_x + (x_n - k), x_n)
        for zh in range(zh_n):
            at = pl.multiple_of((src_x * zh_n + zh) * tile, tile)
            for j in range(col_n):
                to = (zh * col_n + j) * tile
                h_ref[k, to : to + tile, :] = hid_ref[j, pl.ds(at, tile), :]
        turned = h_ref[k].T
        loads[k].wait()
        blk = x_buf[k].reshape(-1, 2, tile, x_ref.shape[-1])
        rows = blk.shape[0] * tile
        acc_out += dot_nn(turned[:part], blk[:, 1].reshape(rows, -1))
        acc_in += dot_nn(turned[part:], blk[:, 0].reshape(rows, -1))
    win_ref[...] = acc_in.astype(bf16)
    wout_ref[...] = acc_out.astype(bf16)


def in_vmem(x):
    return pltpu.with_memory_space_constraint(x, pltpu.VMEM)


def final_body(parts_ref, first_ref, second_ref):
    n, _, wide = parts_ref.shape
    total = parts_ref[0].astype(f32)
    for j in range(1, n):
        total = total + parts_ref[j].astype(f32)
    first_ref[...] = total[:, : wide // 2].astype(bf16)
    second_ref[...] = total[:, wide // 2 :].astype(bf16)


def final_stage(parts):
    _, tile, wide = parts.shape
    vmem = pl.BlockSpec(memory_space=pltpu.VMEM)
    half = jax.ShapeDtypeStruct((tile, wide // 2), bf16)
    return pl.pallas_call(
        final_body, in_specs=[vmem], out_specs=(vmem, vmem), out_shape=(half, half), compiler_params=pltpu.CompilerParams(vmem_limit_bytes=4 << 20), name="final_stage"
    )(in_vmem(parts))


def weight_stage(chunks, hid, dep_n):
    _, _, wide = hid.shape
    d_loc = chunks[0].shape[-1]
    vmem = pl.BlockSpec(memory_space=pltpu.VMEM)
    return pl.pallas_call(
        weight_body,
        in_specs=[pl.BlockSpec(memory_space=pl.ANY)] * 4 + [vmem],
        out_specs=(vmem, vmem, vmem),
        out_shape=(
            jax.ShapeDtypeStruct((wide // 2, d_loc), bf16),
            jax.ShapeDtypeStruct((wide // 2, d_loc), bf16),
            jax.ShapeDtypeStruct((wide * dep_n // 256, 128), f32),
        ),
        scratch_shapes=[
            pltpu.VMEM((1, wide * dep_n // 2), f32),
            pltpu.VMEM((len(chunks), chunks[0].shape[0] // 2, wide), bf16),
            pltpu.VMEM((len(chunks),) + chunks[0].shape, bf16),
            pltpu.SemaphoreType.DMA((len(chunks),)),
        ],
        compiler_params=pltpu.CompilerParams(vmem_limit_bytes=16 << 20), name="weight_stage",
    )(*chunks, in_vmem(hid))


def step(tokens, out_grad, w_in, b_in, w_out):
    y_n, x_n = lax.axis_size("y"), lax.axis_size("x")
    zh_n = lax.axis_size("zh")
    dep_n = zh_n * x_n
    half = dep_n // 2
    tile, d_loc = tokens.shape
    f_loc = w_in.shape[1]
    part = f_loc // dep_n
    my_core = lax.axis_index("core")
    swap = [(0, 1), (1, 0)]

    both = jnp.concatenate([tokens, out_grad], axis=0)
    zall = lax.all_gather(both, ("zh", "zq", "zp"), axis=0, tiled=True)
    others = []
    for k in range(1, x_n):
        others.append(lax.ppermute(zall, "x", [(i, (i + k) % x_n) for i in range(x_n)]))
    mine = zall.reshape(zh_n, y_n, 2, 2, tile, d_loc)

    def first_products(core, kind):
        blk = lax.dynamic_index_in_dim(mine, core, 2, keepdims=False).transpose(2, 1, 0, 3, 4)
        blk = blk.reshape(2, y_n * zh_n * tile, d_loc)
        part_in = dot_nn(blk[0], w_in).astype(kind)
        part_out = dot_nt(blk[1], w_out).astype(kind)
        return jnp.concatenate([part_in, part_out], axis=1)

    from_core = lax.ppermute(first_products(1 - my_core, bf16), "core", swap)
    pre = (first_products(my_core, f32) + from_core.astype(f32)).astype(bf16)
    pre = lax.all_to_all(pre.reshape(y_n, zh_n * tile, 2 * f_loc), "y", 0, 0)
    hid, send = gelu_stage(pre, b_in, zh_n, x_n)
    got = lax.all_to_all(send, "x", 0, 0)
    rows = lax.all_gather(hid, ("y", "core"), axis=0, tiled=True)
    outs = jnp.concatenate(
        [dot_nn(rows[:, :f_loc], w_out).astype(bf16), dot_nt(rows[:, f_loc:], w_in).astype(bf16)],
        axis=1,
    )
    outs = lax.all_to_all(outs.reshape(2 * y_n, tile, 2 * d_loc), ("zq", "zp"), 0, 0)
    block_out, tokens_grad = final_stage(outs)

    tall = zh_n * tile
    b_sum = jnp.sum(got[:, tall : tall + half].astype(f32) + got[:, tall + half :].astype(f32), axis=0)
    b_pair = jnp.concatenate(hi_lo(b_sum), axis=0)
    wsend = jnp.concatenate([got[:, :tall].reshape(dep_n * tile, 2 * part), b_pair], axis=0)
    wall = lax.all_gather(wsend, ("y", "core"), axis=0, tiled=False)
    w_in_grad, w_out_grad, b_in_grad = weight_stage([zall] + others, wall, dep_n)
    return (block_out, tokens_grad, w_in_grad.T, w_out_grad, b_in_grad.reshape(f_loc))


def solution(mesh):
    fine = Mesh(mesh.devices.reshape(fine_shape), fine_names)
    col = ("zq", "zp")
    row = ("y", "core")
    owner = ("zq", "zp", "zh", "x")
    tok = P(owner, row)
    return jax.shard_map(
        step,
        mesh=fine,
        in_specs=(tok, tok, P(row, col), P(col), P(col, row)),
        out_specs=(tok, tok, P(row, owner), P(owner, row), P(col)),
        check_vma=False,
    )
```

```python
import functools

import jax
import jax.numpy as jnp
from jax import lax
from jax.experimental import pallas as pl
from jax.experimental.pallas import tpu as pltpu
from jax.sharding import Mesh, PartitionSpec as P


root_coeff = 0.7978845608028654
cubic_coeff = 0.044715
f32 = jnp.float32
bf16 = jnp.bfloat16
fine_names = ("y", "core", "zq", "zp", "zh", "x")
fine_shape = (4, 2, 4, 2, 2, 4)


def gelu_parts(pre_act):
    inner_arg = root_coeff * (pre_act + cubic_coeff * pre_act * pre_act * pre_act)
    tangent = jnp.tanh(inner_arg)
    gelu_value = 0.5 * pre_act * (1.0 + tangent)
    gelu_slope = 0.5 * (1.0 + tangent) + 0.5 * pre_act * (1.0 - tangent * tangent) * root_coeff * (
        1.0 + 3.0 * cubic_coeff * pre_act * pre_act
    )
    return (gelu_value, gelu_slope)


def dot_nt(a, b):
    return lax.dot_general(a, b, (((1,), (1,)), ((), ())), preferred_element_type=f32)


def dot_nn(a, b):
    return jnp.dot(a, b, preferred_element_type=f32)


def hi_lo(v):
    hi = v.astype(bf16)
    return hi, (v - hi.astype(f32)).astype(bf16)


def gelu_body(zh_n, x_n, recv_ref, bias_ref, hid_ref, send_ref, both_ref):
    y_n, rows_n, wide = recv_ref.shape
    f_loc = wide // 2
    tile = rows_n // zh_n
    far = f_loc // zh_n
    part = far // x_n
    half = f_loc // (2 * part)
    my_zh = lax.axis_index("zh")
    pre = recv_ref[0].astype(f32)
    for j in range(1, y_n):
        pre = pre + recv_ref[j].astype(f32)
    bias = jnp.concatenate([bias_ref[j : j + 1, :] for j in range(bias_ref.shape[0])], axis=1)
    value, slope = gelu_parts(pre[:, :f_loc] + bias)
    pre_grad = pre[:, f_loc:] * slope
    both_ref[:, :f_loc] = value.astype(bf16)
    both_ref[:, f_loc:] = pre_grad.astype(bf16)
    hid_ref[...] = both_ref[pl.ds(pl.multiple_of(my_zh * tile, tile), tile), :]
    rows = jnp.sum(pre_grad, axis=0, keepdims=True)
    high = rows.astype(bf16).astype(f32)
    extra = [v[:, j * 2 * part : (j + 1) * 2 * part] for v in (high, rows - high) for j in range(half)]
    extra = jnp.concatenate(extra, axis=0).astype(bf16)
    near = my_zh == 0
    value = jnp.where(near, value[:, :far], value[:, far:])
    pre_grad = jnp.where(near, pre_grad[:, :far], pre_grad[:, far:])
    for x in range(x_n):
        cut = slice(x * part, (x + 1) * part)
        send_ref[x, :rows_n] = jnp.concatenate([value[:, cut], pre_grad[:, cut]], axis=1).astype(bf16)
        send_ref[x, rows_n:] = extra


def gelu_stage(recv, bias, zh_n, x_n):
    _, rows_n, wide = recv.shape
    dep_n = zh_n * x_n
    vmem = pl.BlockSpec(memory_space=pltpu.VMEM)
    return pl.pallas_call(
        functools.partial(gelu_body, zh_n, x_n),
        in_specs=[vmem, vmem],
        out_specs=(vmem, vmem),
        out_shape=(
            jax.ShapeDtypeStruct((rows_n // zh_n, wide), bf16),
            jax.ShapeDtypeStruct((x_n, rows_n + dep_n, wide // dep_n), bf16),
        ),
        scratch_shapes=[pltpu.VMEM((rows_n, wide), bf16)],
        compiler_params=pltpu.CompilerParams(vmem_limit_bytes=16 << 20),
        name="gelu_stage",
    )(in_vmem(recv), bias.reshape(-1, 128))


def weight_body(x0_ref, x1_ref, x2_ref, x3_ref, hid_ref, win_ref, wout_ref, b_ref, flat_ref, h_ref, x_buf, sem):
    col_n, tall, wide = hid_ref.shape
    part = wide // 2
    half = flat_ref.shape[1] // wide
    dep_n = 2 * half
    tile = (tall - dep_n) // dep_n
    x_refs = (x0_ref, x1_ref, x2_ref, x3_ref)
    x_n = len(x_refs)
    zh_n = dep_n // x_n
    my_x = lax.axis_index("x")
    loads = [pltpu.make_async_copy(x_ref, x_buf.at[k], sem.at[k]) for k, x_ref in enumerate(x_refs)]
    for load in loads:
        load.start()
    total = jnp.zeros((dep_n, wide), f32)
    for j in range(col_n):
        total = total + hid_ref[j, dep_n * tile :].astype(f32)
    total = total[:half] + total[half:]
    for j in range(half):
        flat_ref[:, j * wide : (j + 1) * wide] = total[j : j + 1]
    for j in range(b_ref.shape[0]):
        b_ref[j : j + 1, :] = flat_ref[:, j * 128 : (j + 1) * 128]
    acc_in = jnp.zeros(win_ref.shape, f32)
    acc_out = jnp.zeros(wout_ref.shape, f32)
    for k, x_ref in enumerate(x_refs):
        src_x = lax.rem(my_x + (x_n - k), x_n)
        for zh in range(zh_n):
            at = pl.multiple_of((src_x * zh_n + zh) * tile, tile)
            for j in range(col_n):
                to = (zh * col_n + j) * tile
                h_ref[k, to : to + tile, :] = hid_ref[j, pl.ds(at, tile), :]
        turned = h_ref[k].T
        loads[k].wait()
        blk = x_buf[k].reshape(-1, 2, tile, x_ref.shape[-1])
        rows = blk.shape[0] * tile
        acc_out += dot_nn(turned[:part], blk[:, 1].reshape(rows, -1))
        acc_in += dot_nn(turned[part:], blk[:, 0].reshape(rows, -1))
    win_ref[...] = acc_in.astype(bf16)
    wout_ref[...] = acc_out.astype(bf16)


def in_vmem(x):
    return pltpu.with_memory_space_constraint(x, pltpu.VMEM)


def product_body(rows_ref, win_ref, wout_ref, out_ref, win_buf, sem):
    load = pltpu.make_async_copy(win_ref, win_buf, sem.at[0])
    load.start()
    n, tile, wide = out_ref.shape
    f_loc = rows_ref.shape[1] // 2
    first = dot_nn(rows_ref[:, :f_loc], wout_ref[...]).astype(bf16)
    out_ref[:, :, : wide // 2] = first.reshape(n, tile, wide // 2)
    load.wait()
    second = dot_nt(rows_ref[:, f_loc:], win_buf[...]).astype(bf16)
    out_ref[:, :, wide // 2 :] = second.reshape(n, tile, wide // 2)


def product_stage(rows, w_in, w_out, tile):
    vmem = pl.BlockSpec(memory_space=pltpu.VMEM)
    return pl.pallas_call(
        product_body,
        in_specs=[vmem, pl.BlockSpec(memory_space=pl.ANY), vmem],
        out_specs=vmem,
        out_shape=jax.ShapeDtypeStruct((rows.shape[0] // tile, tile, 2 * w_in.shape[0]), bf16),
        scratch_shapes=[pltpu.VMEM(w_in.shape, bf16), pltpu.SemaphoreType.DMA((1,))],
        compiler_params=pltpu.CompilerParams(vmem_limit_bytes=16 << 20),
        name="product_stage",
    )(in_vmem(rows), w_in, in_vmem(w_out))


def final_body(parts_ref, first_ref, second_ref):
    n, _, wide = parts_ref.shape
    total = parts_ref[0].astype(f32)
    for j in range(1, n):
        total = total + parts_ref[j].astype(f32)
    first_ref[...] = total[:, : wide // 2].astype(bf16)
    second_ref[...] = total[:, wide // 2 :].astype(bf16)


def final_stage(parts):
    _, tile, wide = parts.shape
    vmem = pl.BlockSpec(memory_space=pltpu.VMEM)
    half = jax.ShapeDtypeStruct((tile, wide // 2), bf16)
    return pl.pallas_call(
        final_body, in_specs=[vmem], out_specs=(vmem, vmem), out_shape=(half, half), compiler_params=pltpu.CompilerParams(vmem_limit_bytes=4 << 20), name="final_stage"
    )(in_vmem(parts))


def weight_stage(chunks, hid, dep_n):
    _, _, wide = hid.shape
    d_loc = chunks[0].shape[-1]
    vmem = pl.BlockSpec(memory_space=pltpu.VMEM)
    return pl.pallas_call(
        weight_body,
        in_specs=[pl.BlockSpec(memory_space=pl.ANY)] * 4 + [vmem],
        out_specs=(vmem, vmem, vmem),
        out_shape=(
            jax.ShapeDtypeStruct((wide // 2, d_loc), bf16),
            jax.ShapeDtypeStruct((wide // 2, d_loc), bf16),
            jax.ShapeDtypeStruct((wide * dep_n // 256, 128), f32),
        ),
        scratch_shapes=[
            pltpu.VMEM((1, wide * dep_n // 2), f32),
            pltpu.VMEM((len(chunks), chunks[0].shape[0] // 2, wide), bf16),
            pltpu.VMEM((len(chunks),) + chunks[0].shape, bf16),
            pltpu.SemaphoreType.DMA((len(chunks),)),
        ],
        compiler_params=pltpu.CompilerParams(vmem_limit_bytes=16 << 20), name="weight_stage",
    )(*chunks, in_vmem(hid))


def step(tokens, out_grad, w_in, b_in, w_out):
    y_n, x_n = lax.axis_size("y"), lax.axis_size("x")
    zh_n = lax.axis_size("zh")
    dep_n = zh_n * x_n
    half = dep_n // 2
    tile, d_loc = tokens.shape
    f_loc = w_in.shape[1]
    part = f_loc // dep_n
    my_core = lax.axis_index("core")
    swap = [(0, 1), (1, 0)]

    both = jnp.concatenate([tokens, out_grad], axis=0)
    zall = lax.all_gather(both, ("zh", "zq", "zp"), axis=0, tiled=True)
    others = []
    for k in range(1, x_n):
        others.append(lax.ppermute(zall, "x", [(i, (i + k) % x_n) for i in range(x_n)]))
    mine = zall.reshape(zh_n, y_n, 2, 2, tile, d_loc)

    def first_products(core, kind):
        blk = lax.dynamic_index_in_dim(mine, core, 2, keepdims=False).transpose(2, 1, 0, 3, 4)
        blk = blk.reshape(2, y_n * zh_n * tile, d_loc)
        part_in = dot_nn(blk[0], w_in).astype(kind)
        part_out = dot_nt(blk[1], w_out).astype(kind)
        return jnp.concatenate([part_in, part_out], axis=1)

    from_core = lax.ppermute(first_products(1 - my_core, bf16), "core", swap)
    pre = (first_products(my_core, f32) + from_core.astype(f32)).astype(bf16)
    pre = lax.all_to_all(pre.reshape(y_n, zh_n * tile, 2 * f_loc), "y", 0, 0)
    hid, send = gelu_stage(pre, b_in, zh_n, x_n)
    got = lax.all_to_all(send, "x", 0, 0)
    rows = lax.all_gather(hid, ("y", "core"), axis=0, tiled=True)
    outs = product_stage(rows, w_in, w_out, tile)
    outs = lax.all_to_all(outs, ("zq", "zp"), 0, 0)
    block_out, tokens_grad = final_stage(outs)

    tall = zh_n * tile
    b_sum = jnp.sum(got[:, tall : tall + half].astype(f32) + got[:, tall + half :].astype(f32), axis=0)
    b_pair = jnp.concatenate(hi_lo(b_sum), axis=0)
    wsend = jnp.concatenate([got[:, :tall].reshape(dep_n * tile, 2 * part), b_pair], axis=0)
    wall = lax.all_gather(wsend, ("y", "core"), axis=0, tiled=False)
    w_in_grad, w_out_grad, b_in_grad = weight_stage([zall] + others, wall, dep_n)
    return (block_out, tokens_grad, w_in_grad.T, w_out_grad, b_in_grad.reshape(f_loc))


def solution(mesh):
    fine = Mesh(mesh.devices.reshape(fine_shape), fine_names)
    col = ("zq", "zp")
    row = ("y", "core")
    owner = ("zq", "zp", "zh", "x")
    tok = P(owner, row)
    return jax.shard_map(
        step,
        mesh=fine,
        in_specs=(tok, tok, P(row, col), P(col), P(col, row)),
        out_specs=(tok, tok, P(row, owner), P(owner, row), P(col)),
        check_vma=False,
    )
```

```python
import functools

import jax
import jax.numpy as jnp
from jax import lax
from jax.experimental import pallas as pl
from jax.experimental.pallas import tpu as pltpu
from jax.sharding import Mesh, PartitionSpec as P


root_coeff = 0.7978845608028654
cubic_coeff = 0.044715
f32 = jnp.float32
bf16 = jnp.bfloat16
fine_names = ("y", "core", "zq", "zp", "zh", "x")
fine_shape = (4, 2, 4, 2, 2, 4)


def gelu_parts(pre_act):
    inner_arg = root_coeff * (pre_act + cubic_coeff * pre_act * pre_act * pre_act)
    tangent = jnp.tanh(inner_arg)
    gelu_value = 0.5 * pre_act * (1.0 + tangent)
    gelu_slope = 0.5 * (1.0 + tangent) + 0.5 * pre_act * (1.0 - tangent * tangent) * root_coeff * (
        1.0 + 3.0 * cubic_coeff * pre_act * pre_act
    )
    return (gelu_value, gelu_slope)


def dot_nt(a, b):
    return lax.dot_general(a, b, (((1,), (1,)), ((), ())), preferred_element_type=f32)


def dot_nn(a, b):
    return jnp.dot(a, b, preferred_element_type=f32)


def hi_lo(v):
    hi = v.astype(bf16)
    return hi, (v - hi.astype(f32)).astype(bf16)


def gelu_body(zh_n, x_n, recv_ref, bias_ref, hid_ref, send_ref, both_ref):
    y_n, rows_n, wide = recv_ref.shape
    f_loc = wide // 2
    tile = rows_n // zh_n
    far = f_loc // zh_n
    part = far // x_n
    half = f_loc // (2 * part)
    my_zh = lax.axis_index("zh")
    pre = recv_ref[0].astype(f32)
    for j in range(1, y_n):
        pre = pre + recv_ref[j].astype(f32)
    bias = jnp.concatenate([bias_ref[j : j + 1, :] for j in range(bias_ref.shape[0])], axis=1)
    value, slope = gelu_parts(pre[:, :f_loc] + bias)
    pre_grad = pre[:, f_loc:] * slope
    both_ref[:, :f_loc] = value.astype(bf16)
    both_ref[:, f_loc:] = pre_grad.astype(bf16)
    hid_ref[...] = both_ref[pl.ds(pl.multiple_of(my_zh * tile, tile), tile), :]
    rows = jnp.sum(pre_grad, axis=0, keepdims=True)
    high = rows.astype(bf16).astype(f32)
    extra = [v[:, j * 2 * part : (j + 1) * 2 * part] for v in (high, rows - high) for j in range(half)]
    extra = jnp.concatenate(extra, axis=0).astype(bf16)
    near = my_zh == 0
    value = jnp.where(near, value[:, :far], value[:, far:])
    pre_grad = jnp.where(near, pre_grad[:, :far], pre_grad[:, far:])
    for x in range(x_n):
        cut = slice(x * part, (x + 1) * part)
        send_ref[x, :rows_n] = jnp.concatenate([value[:, cut], pre_grad[:, cut]], axis=1).astype(bf16)
        send_ref[x, rows_n:] = extra


def gelu_stage(recv, bias, zh_n, x_n):
    _, rows_n, wide = recv.shape
    dep_n = zh_n * x_n
    vmem = pl.BlockSpec(memory_space=pltpu.VMEM)
    return pl.pallas_call(
        functools.partial(gelu_body, zh_n, x_n),
        in_specs=[vmem, vmem],
        out_specs=(vmem, vmem),
        out_shape=(
            jax.ShapeDtypeStruct((rows_n // zh_n, wide), bf16),
            jax.ShapeDtypeStruct((x_n, rows_n + dep_n, wide // dep_n), bf16),
        ),
        scratch_shapes=[pltpu.VMEM((rows_n, wide), bf16)],
        compiler_params=pltpu.CompilerParams(vmem_limit_bytes=16 << 20),
        name="gelu_stage",
    )(in_vmem(recv), bias.reshape(-1, 128))


def weight_body(x0_ref, x1_ref, x2_ref, x3_ref, hid_ref, win_ref, wout_ref, b_ref, flat_ref, h_ref, x_buf, sem):
    col_n, tall, wide = hid_ref.shape
    part = wide // 2
    half = flat_ref.shape[1] // wide
    dep_n = 2 * half
    tile = (tall - dep_n) // dep_n
    x_refs = (x0_ref, x1_ref, x2_ref, x3_ref)
    x_n = len(x_refs)
    zh_n = dep_n // x_n
    my_x = lax.axis_index("x")
    loads = [pltpu.make_async_copy(x_ref, x_buf.at[k], sem.at[k]) for k, x_ref in enumerate(x_refs)]
    for load in loads:
        load.start()
    total = jnp.zeros((dep_n, wide), f32)
    for j in range(col_n):
        total = total + hid_ref[j, dep_n * tile :].astype(f32)
    total = total[:half] + total[half:]
    for j in range(half):
        flat_ref[:, j * wide : (j + 1) * wide] = total[j : j + 1]
    for j in range(b_ref.shape[0]):
        b_ref[j : j + 1, :] = flat_ref[:, j * 128 : (j + 1) * 128]
    acc_in = jnp.zeros(win_ref.shape, f32)
    acc_out = jnp.zeros(wout_ref.shape, f32)
    for k, x_ref in enumerate(x_refs):
        src_x = lax.rem(my_x + (x_n - k), x_n)
        for zh in range(zh_n):
            at = pl.multiple_of((src_x * zh_n + zh) * tile, tile)
            for j in range(col_n):
                to = (zh * col_n + j) * tile
                h_ref[k, to : to + tile, :] = hid_ref[j, pl.ds(at, tile), :]
        turned = h_ref[k].T
        loads[k].wait()
        blk = x_buf[k].reshape(-1, 2, tile, x_ref.shape[-1])
        rows = blk.shape[0] * tile
        acc_out += dot_nn(turned[:part], blk[:, 1].reshape(rows, -1))
        acc_in += dot_nn(turned[part:], blk[:, 0].reshape(rows, -1))
    win_ref[...] = acc_in.astype(bf16)
    wout_ref[...] = acc_out.astype(bf16)


def in_vmem(x):
    return pltpu.with_memory_space_constraint(x, pltpu.VMEM)


def final_body(parts_ref, first_ref, second_ref):
    n, _, wide = parts_ref.shape
    total = parts_ref[0].astype(f32)
    for j in range(1, n):
        total = total + parts_ref[j].astype(f32)
    first_ref[...] = total[:, : wide // 2].astype(bf16)
    second_ref[...] = total[:, wide // 2 :].astype(bf16)


def final_stage(parts):
    _, tile, wide = parts.shape
    vmem = pl.BlockSpec(memory_space=pltpu.VMEM)
    half = jax.ShapeDtypeStruct((tile, wide // 2), bf16)
    return pl.pallas_call(
        final_body, in_specs=[vmem], out_specs=(vmem, vmem), out_shape=(half, half), compiler_params=pltpu.CompilerParams(vmem_limit_bytes=4 << 20), name="final_stage"
    )(in_vmem(parts))


def weight_stage(chunks, hid, dep_n):
    _, _, wide = hid.shape
    d_loc = chunks[0].shape[-1]
    vmem = pl.BlockSpec(memory_space=pltpu.VMEM)
    return pl.pallas_call(
        weight_body,
        in_specs=[pl.BlockSpec(memory_space=pl.ANY)] * 4 + [vmem],
        out_specs=(vmem, vmem, vmem),
        out_shape=(
            jax.ShapeDtypeStruct((wide // 2, d_loc), bf16),
            jax.ShapeDtypeStruct((wide // 2, d_loc), bf16),
            jax.ShapeDtypeStruct((wide * dep_n // 256, 128), f32),
        ),
        scratch_shapes=[
            pltpu.VMEM((1, wide * dep_n // 2), f32),
            pltpu.VMEM((len(chunks), chunks[0].shape[0] // 2, wide), bf16),
            pltpu.VMEM((len(chunks),) + chunks[0].shape, bf16),
            pltpu.SemaphoreType.DMA((len(chunks),)),
        ],
        compiler_params=pltpu.CompilerParams(vmem_limit_bytes=16 << 20), name="weight_stage",
    )(*chunks, in_vmem(hid))


def step(tokens, out_grad, w_in, b_in, w_out):
    y_n, x_n = lax.axis_size("y"), lax.axis_size("x")
    zh_n = lax.axis_size("zh")
    dep_n = zh_n * x_n
    half = dep_n // 2
    tile, d_loc = tokens.shape
    f_loc = w_in.shape[1]
    part = f_loc // dep_n
    my_core = lax.axis_index("core")
    swap = [(0, 1), (1, 0)]

    both = jnp.concatenate([tokens, out_grad], axis=0)
    zall = lax.all_gather(both, ("zh", "zq", "zp"), axis=0, tiled=True)
    others = []
    for k in range(1, x_n):
        others.append(lax.ppermute(zall, "x", [(i, (i + k) % x_n) for i in range(x_n)]))
    mine = zall.reshape(zh_n, y_n, 2, 2, tile, d_loc)

    def first_products(core, kind):
        blk = lax.dynamic_index_in_dim(mine, core, 2, keepdims=False).transpose(2, 1, 0, 3, 4)
        blk = blk.reshape(2, y_n * zh_n * tile, d_loc)
        part_in = dot_nn(blk[0], w_in).astype(kind)
        part_out = dot_nt(blk[1], w_out).astype(kind)
        return jnp.concatenate([part_in, part_out], axis=1)

    from_core = lax.ppermute(first_products(1 - my_core, bf16), "core", swap)
    pre = (first_products(my_core, f32) + from_core.astype(f32)).astype(bf16)
    pre = lax.all_to_all(pre.reshape(y_n, zh_n * tile, 2 * f_loc), "y", 0, 0)
    hid, send = gelu_stage(pre, b_in, zh_n, x_n)
    got = lax.all_to_all(send, "x", 0, 0)
    rows = lax.all_gather(hid, ("y", "core"), axis=0, tiled=True)
    first = dot_nn(rows[:, :f_loc], w_out).astype(bf16)
    second = dot_nt(rows[:, f_loc:], w_in).astype(bf16)
    outs = lax.optimization_barrier(jnp.zeros((rows.shape[0], 2 * d_loc), bf16))
    outs = lax.dynamic_update_slice(outs, second, (0, d_loc))
    outs = lax.dynamic_update_slice(outs, first, (0, 0))
    outs = lax.all_to_all(outs.reshape(2 * y_n, tile, 2 * d_loc), ("zq", "zp"), 0, 0)
    block_out, tokens_grad = final_stage(outs)

    tall = zh_n * tile
    b_sum = jnp.sum(got[:, tall : tall + half].astype(f32) + got[:, tall + half :].astype(f32), axis=0)
    b_pair = jnp.concatenate(hi_lo(b_sum), axis=0)
    wsend = jnp.concatenate([got[:, :tall].reshape(dep_n * tile, 2 * part), b_pair], axis=0)
    wall = lax.all_gather(wsend, ("y", "core"), axis=0, tiled=False)
    w_in_grad, w_out_grad, b_in_grad = weight_stage([zall] + others, wall, dep_n)
    return (block_out, tokens_grad, w_in_grad.T, w_out_grad, b_in_grad.reshape(f_loc))


def solution(mesh):
    fine = Mesh(mesh.devices.reshape(fine_shape), fine_names)
    col = ("zq", "zp")
    row = ("y", "core")
    owner = ("zq", "zp", "zh", "x")
    tok = P(owner, row)
    return jax.shard_map(
        step,
        mesh=fine,
        in_specs=(tok, tok, P(row, col), P(col), P(col, row)),
        out_specs=(tok, tok, P(row, owner), P(owner, row), P(col)),
        check_vma=False,
    )
```
